32 devices in a mesh: groups: 2 (over y), replica: 1, da: 4 (over x, core), db: 4 (over z).
Axes of the slice: x: 2, y: 2, z: 4, core: 2. Of those that a mesh axis runs over, the one named last changes fastest.
Arguments:
- tokens: bfloat16 [4096, 1024], P(('groups', 'replica', 'da', 'db')), parts along dimension 0, may hold values from -6 to 6
- grad_out: bfloat16 [4096, 1024], P(('groups', 'replica', 'da', 'db')), parts along dimension 0, may hold values from -3 to 3
- routes: int32 [4096, 8], P(('groups', 'replica', 'da', 'db')), parts along dimension 0, may hold values from 0 to 15, as said below
- gates: bfloat16 [4096, 8], P(('groups', 'replica', 'da', 'db')), parts along dimension 0, may hold values from 0.019897461 to 0.5
- w_gate_up: bfloat16 [16, 1024, 768], P(('da', 'db'), 'replica'), may hold values from -0.1875 to 0.1875
- w_down: bfloat16 [16, 384, 1024], P(('da', 'db'), 'replica'), may hold values from -0.3125 to 0.3125
Outputs:
- token_grads: bfloat16 [4096, 1024], P(('groups', 'replica', 'da', 'db')), parts along dimension 0
- gate_grads: bfloat16 [4096, 8], P(('groups', 'replica', 'da', 'db')), parts along dimension 0
- gate_up_grads: bfloat16 [32, 1024, 768], P(('groups', 'da', 'db'), 'replica'), parts along dimension 0
- down_grads: bfloat16 [32, 384, 1024], P(('groups', 'da', 'db'), 'replica'), parts along dimension 0
The draws below stay inside these ranges and needn't reach their ends.
There are 2 independent parts, one for each index of `groups`. The reference program is written for one: setup_inputs(seed, part) draws one part's arguments, and reference() takes and returns one part's arrays. A program takes and returns all parts, laid end to end along the dimension named above; an argument that names none is the same for every part. Nothing has to cross between parts.
Inputs may be any that keep to these rules, and one draw needn't show every extreme that they name: `routes`: each token names 8 different experts. In every aligned block of 2 consecutive tokens, each expert is named exactly once, so the tokens of one device name every expert exactly 64 times.
All inputs are finite; a program needn't handle non-finite values.
Results may differ from the reference program's by a relative error of at most 0.0085.
Values may be sent and summed in bfloat16 or wider, within the bound.
A program may use at most 64 MiB of HBM per device.

```python
import math
import jax
import jax.numpy as jnp
from jax import lax

D = 1024
FF = 384
TOP = 8
TOK_DEV = 128
EXPERTS = 16
TOKENS = 2048
N_REPLICA = 1
N_DA = 4
N_DB = 4


def draw_routes(key, part):
    per_round = EXPERTS // TOP
    round_count = TOKENS // per_round
    keys = jax.random.split(jax.random.fold_in(key, 7), round_count)
    orders = jax.vmap(lambda one: jax.random.permutation(one, EXPERTS))(keys)
    return orders.reshape(TOKENS, TOP).astype(jnp.int32)


def block_levels(stream_key, shape, shards, least, top_value):
    def one(dim, shards_of):
        heights = jax.random.uniform(jax.random.fold_in(jax.random.fold_in(stream_key, 6), dim), (shards_of,), jnp.float32, least / len(shards), top_value / len(shards))
        return jnp.repeat(jnp.exp(heights), shape[dim] // shards_of).reshape((-1,) + (1,) * (len(shape) - dim - 1))

    loudness = one(*shards[0])
    for cut in shards[1:]:
        loudness = loudness * one(*cut)
    return loudness


def centred(own_key, extent, spread, most, cuts=(), held_as=jnp.bfloat16):
    array = jax.random.normal(own_key, extent, jnp.float32) * spread
    if len(cuts) > 0:
        array = block_levels(own_key, extent, cuts, -0.22, 0.18) * array
    return jnp.clip(array, min=-most, max=most).astype(held_as)


def setup_inputs(seed: int = 0, part: int = 0) -> dict:
    splits = jax.random.split(jax.random.key(seed), 7)
    own_keys = jax.random.split(jax.random.fold_in(splits[6], part), 7)
    return {
        "tokens": centred(own_keys[0], (TOKENS, D), 1.0, 6.0, ((0, 16),)),
        "grad_out": centred(own_keys[1], (TOKENS, D), 0.5, 3.0, ((0, 16),)),
        "routes": draw_routes(jax.random.fold_in(jax.random.fold_in(splits[6], part), 71), part),
        "gates": jnp.clip(jnp.exp(math.log(0.5) - 3.224016 * jax.random.uniform(own_keys[3], (TOKENS, TOP), jnp.float32) ** block_levels(own_keys[3], (TOKENS, TOP), ((0, 16),), -0.2, 0.2)), 0.019897461, 0.5).astype(jnp.bfloat16),
        "w_gate_up": centred(splits[4], (EXPERTS, D, 2 * FF), D ** -0.5, 0.1875, ((0, 16),)),
        "w_down": centred(splits[5], (EXPERTS, FF, D), FF ** -0.5, 0.3125, ((0, 16),)),
    }


def silu_parts(projected):
    sigmoid = jax.nn.sigmoid(projected)
    return projected * sigmoid, sigmoid * (1.0 + projected * (1.0 - sigmoid))


def replica_sum(partials):
    rounded = lax.optimization_barrier(partials.astype(jnp.bfloat16))
    return jnp.sum(rounded.astype(jnp.float32), axis=0).astype(jnp.bfloat16)


def reference(tokens, grad_out, routes, gates, w_gate_up, w_down):
    per_replica = TOK_DEV * N_DA * N_DB
    flat_routes = routes.reshape(N_REPLICA, per_replica * TOP)
    ordering = jnp.argsort(flat_routes, axis=1, stable=True).astype(jnp.int32)
    rows_expert = per_replica * TOP // EXPERTS
    ordering = ordering.reshape(N_REPLICA, EXPERTS, rows_expert)
    offsets = (jnp.arange(N_REPLICA, dtype=jnp.int32) * (per_replica * TOP)).astype(jnp.int32)
    route_index = (ordering + offsets[:, None, None]).astype(jnp.int32)
    route_index = jnp.transpose(route_index, (1, 0, 2))
    flat_gates = gates.reshape(-1)

    def expert_step(carry, inputs):
        token_acc, gate_acc = carry
        index, w_in, w_out = inputs
        token_ids = (index // TOP).astype(jnp.int32)
        input_rows = tokens[token_ids].astype(jnp.float32)
        upstream = grad_out[token_ids].astype(jnp.float32)
        gate_rows = flat_gates[index].astype(jnp.float32)[..., None]
        w_in_f = w_in.astype(jnp.float32)
        w_out_f = w_out.astype(jnp.float32)
        projected = jnp.einsum("prd,df->prf", input_rows, w_in_f)
        gate_part = projected[..., :FF]
        up_part = projected[..., FF:]
        activated, derivative = silu_parts(gate_part)
        hidden = (activated * up_part).astype(jnp.bfloat16)
        back_raw = jnp.einsum("prd,fd->prf", upstream, w_out_f)
        gate_scores = jnp.sum(hidden.astype(jnp.float32) * back_raw, axis=-1).astype(jnp.bfloat16)
        back_hidden = gate_rows * back_raw
        grad_projected = jnp.concatenate([back_hidden * up_part * derivative, back_hidden * activated], axis=-1).astype(jnp.bfloat16)
        scaled_upstream = (gate_rows * upstream).astype(jnp.bfloat16)
        input_grads = jnp.einsum("prf,df->prd", grad_projected.astype(jnp.float32), w_in_f).astype(jnp.bfloat16)
        grad_in = replica_sum(jnp.einsum("prd,prf->pdf", input_rows, grad_projected.astype(jnp.float32)))
        grad_down = replica_sum(jnp.einsum("prf,prd->pfd", hidden.astype(jnp.float32), scaled_upstream.astype(jnp.float32)))
        token_acc = token_acc.at[token_ids.reshape(-1)].add(input_grads.reshape(-1, D).astype(jnp.float32))
        gate_acc = gate_acc.at[index.reshape(-1)].set(gate_scores.reshape(-1))
        return (token_acc, gate_acc), (grad_in, grad_down)

    start = (jnp.zeros((TOKENS, D), jnp.float32), jnp.zeros((TOKENS * TOP,), jnp.bfloat16))
    (token_acc, gate_acc), (gate_up_grads, down_grads) = lax.scan(expert_step, start, (route_index, w_gate_up, w_down))
    return token_acc.astype(jnp.bfloat16), gate_acc.reshape(TOKENS, TOP), gate_up_grads, down_grads
```

```python
import functools

import jax
import jax.numpy as jnp
from jax import lax
from jax.experimental import pallas as pl
from jax.experimental.pallas import tpu as pltpu
from jax.sharding import PartitionSpec as P


CORES = 2
MESH = pl.DeviceIdType.MESH


def silu_parts(projected):
    sigmoid = jax.nn.sigmoid(projected)
    return (projected * sigmoid, sigmoid * (1.0 + projected * (1.0 - sigmoid)))


def body(tokens, grad_out, routes, gates, w_gate_up, w_down):
    local_tokens, features = tokens.shape
    top_count = routes.shape[1]
    hidden_units = w_gate_up.shape[2] // 2
    first_size = lax.axis_size("da")
    second_size = lax.axis_size("db")
    experts = first_size * second_size
    per_round = experts // top_count
    rounds = local_tokens // per_round
    expert_ids = lax.broadcasted_iota(jnp.int32, (1, 1, 1, experts), 3)
    matches = routes.reshape(rounds, per_round, top_count, 1) == expert_ids
    gate_values = gates.reshape(rounds, per_round, top_count, 1).astype(jnp.float32)
    gate_table = jnp.sum(jnp.where(matches, gate_values, 0.0), axis=(1, 2)).astype(jnp.bfloat16)
    chosen = jnp.any(matches, axis=2).astype(jnp.bfloat16)
    input_send = jnp.einsum(
        "rge,rgd->red",
        chosen,
        tokens.reshape(rounds, per_round, features),
        preferred_element_type=jnp.float32,
    ).astype(jnp.bfloat16)
    upstream_send = jnp.einsum(
        "rge,rgd->red",
        chosen,
        grad_out.reshape(rounds, per_round, features),
        preferred_element_type=jnp.float32,
    ).astype(jnp.bfloat16)
    input_recv, upstream_recv, gate_recv = (
        lax.all_to_all(input_send, ("da", "db"), split_axis=1, concat_axis=1, tiled=True),
        lax.all_to_all(upstream_send, ("da", "db"), split_axis=1, concat_axis=1, tiled=True),
        lax.all_to_all(gate_table, ("da", "db"), split_axis=1, concat_axis=1, tiled=True),
    )
    input_rows = input_recv.reshape(-1, features)
    upstream_rows = upstream_recv.reshape(-1, features)
    gate_rows = gate_recv.reshape(-1, 1).astype(jnp.float32)
    w_in, w_out = (
        lax.all_gather(w_gate_up[0], "replica", axis=0, tiled=True),
        lax.all_gather(w_down[0], "replica", axis=0, tiled=True),
    )
    projected = jnp.dot(input_rows, w_in, preferred_element_type=jnp.float32)
    back_raw = jnp.einsum("rd,fd->rf", upstream_rows, w_out, preferred_element_type=jnp.float32)
    gate_part = projected[:, :hidden_units]
    up_part = projected[:, hidden_units:]
    activated, derivative = silu_parts(gate_part)
    hidden = (activated * up_part).astype(jnp.bfloat16)
    gate_scores = jnp.sum(hidden.astype(jnp.float32) * back_raw, axis=1).astype(jnp.bfloat16)
    back_hidden = gate_rows * back_raw
    grad_projected = jnp.concatenate(
        [back_hidden * up_part * derivative, back_hidden * activated], axis=1
    ).astype(jnp.bfloat16)
    scaled_upstream = (gate_rows * upstream_rows.astype(jnp.float32)).astype(jnp.bfloat16)
    input_grads = jnp.einsum("rf,df->rd", grad_projected, w_in, preferred_element_type=jnp.float32)
    input_grads = input_grads.astype(jnp.bfloat16).reshape(rounds, experts, features)
    score_back = gate_scores.reshape(rounds, experts)
    returned, score_ret = (
        lax.all_to_all(input_grads, ("da", "db"), split_axis=1, concat_axis=1, tiled=True),
        lax.all_to_all(score_back, ("da", "db"), split_axis=1, concat_axis=1, tiled=True),
    )
    score_ret = score_ret.reshape(rounds, 1, 1, experts).astype(jnp.float32)
    token_grads = (
        jnp.einsum("rge,red->rgd", chosen, returned, preferred_element_type=jnp.float32)
        .astype(jnp.bfloat16)
        .reshape(local_tokens, features)
    )
    gate_grads = (
        jnp.sum(jnp.where(matches, score_ret, 0.0), axis=3)
        .astype(jnp.bfloat16)
        .reshape(local_tokens, top_count)
    )
    columns = input_rows
    grad_in = lax.psum_scatter(
        jnp.einsum("rd,rf->df", columns, grad_projected, preferred_element_type=jnp.float32).astype(
            jnp.bfloat16
        ),
        "replica",
        scatter_dimension=0,
        tiled=True,
    )
    columns = hidden
    grad_down = lax.psum_scatter(
        jnp.einsum(
            "rf,rd->fd", columns, scaled_upstream, preferred_element_type=jnp.float32
        ).astype(jnp.bfloat16),
        "replica",
        scatter_dimension=0,
        tiled=True,
    )
    return (token_grads, gate_grads, grad_in[None], grad_down[None])


def visit(j, z, n):
    m = jnp.minimum(z, n - 1 - z)
    near = z + (1 - 2 * (j % 2)) * ((j + 1) // 2)
    far = jnp.where(z < n - 1 - z, j, n - 1 - j)
    return jnp.where(j <= 2 * m, near, far)


def dot(a, b, dims):
    return lax.dot_general(a, b, (dims, ((), ())), preferred_element_type=jnp.float32)


def fused_kernel(
    cols, depth, group,
    tok_hbm, up_hbm, routes_ref, gates_ref, win_hbm, wout_hbm,
    tg_ref, gg_ref, gin_ref, gdown_ref,
    tok, up, table, win, wout, xs, su, hid, gp, igs, igb, ps, pk, pr, rs, rk, rz, scs, scr,
    load_sem, recv_sem, zup_sem, zdn_sem, x_sem, p_sem, igs_sem, igr_sem, ps_sem, pr_sem, rs_sem, rz_sem,
    scs_sem, scr_sem,
):
    da = lax.axis_index("da")
    z = lax.axis_index("db")
    x, c = da // CORES, da % CORES
    local, features = tok.shape[1], tok.shape[2]
    experts = table.shape[1]
    top = routes_ref.shape[1]
    rows = local // group
    ff = wout.shape[0]
    others = cols - 1

    def slot(xx, zz, cc):
        return (xx * CORES + cc) * depth + zz

    me = slot(x, z, c)
    loads = [
        pltpu.make_async_copy(tok_hbm, tok.at[me], load_sem.at[0]),
        pltpu.make_async_copy(up_hbm, up.at[me], load_sem.at[1]),
        pltpu.make_async_copy(win_hbm.at[0], win, load_sem.at[2]),
        pltpu.make_async_copy(wout_hbm.at[0], wout, load_sem.at[3]),
    ]
    for one in loads:
        one.start()

    barrier = pltpu.get_barrier_semaphore()
    count = cols * CORES * depth

    @pl.loop(1, count)
    def _(k):
        to = (me + k) % count
        pl.semaphore_signal(
            barrier, inc=1, device_id={"da": to // depth, "db": to % depth}, device_id_type=MESH
        )

    routes = routes_ref[...]
    gates = gates_ref[...].astype(jnp.float32)
    lanes = lax.broadcasted_iota(jnp.int32, (local, local), 1)
    chart = jnp.zeros((local, local), jnp.float32)
    for k in range(top):
        chart = chart + jnp.where(routes[:, k : k + 1] == lanes, gates[:, k : k + 1], 0.0)
    table[me] = chart.T[:experts].astype(jnp.bfloat16)

    pl.semaphore_wait(barrier, count - 1)
    loads[0].wait()
    loads[1].wait()

    held = (table, tok, up)

    def send(src, dst, send_sem, recv, to_x, to_z, to_c):
        return pltpu.make_async_remote_copy(
            src_ref=src,
            dst_ref=dst,
            send_sem=send_sem,
            recv_sem=recv,
            device_id={"da": to_x * CORES + to_c, "db": to_z},
            device_id_type=MESH,
        )

    def relay(s, a, sem, to_x, to_z, to_c):
        ref = held[a].at[s]
        return send(ref, ref, sem, recv_sem.at[s, a], to_x, to_z, to_c)

    def arrive(s):
        for a in range(3):
            relay(s, a, p_sem.at[0, 0, a], x, z, 1 - c).wait_recv()

    def spread_column(zz, act):
        s = slot(x, zz, c)

        @pl.when((zz <= z) & (z < depth - 1))
        def _():
            for a in range(3):
                act(relay(s, a, zup_sem.at[zz, a], x, z + 1, c))

        @pl.when((zz >= z) & (z > 0))
        def _():
            for a in range(3):
                act(relay(s, a, zdn_sem.at[zz, a], x, z - 1, c))

        for a in range(3):
            for o in range(others):
                act(relay(s, a, x_sem.at[o, zz, a], (x + 1 + o) % cols, z, c))
        for a in range(3):
            act(relay(s, a, p_sem.at[0, zz, a], x, z, 1 - c))

    def spread_core(o, zz, act):
        s = slot((x + 1 + o) % cols, zz, c)
        for a in range(3):
            act(relay(s, a, p_sem.at[1 + o, zz, a], x, z, 1 - c))

    def pick(s, e):
        chart_s = table[s].astype(jnp.float32)
        which = lax.broadcasted_iota(jnp.int32, chart_s.shape, 0) == e
        row = jnp.sum(jnp.where(which, chart_s, 0.0), axis=0, keepdims=True)
        off = lax.broadcasted_iota(jnp.int32, (rows, local), 1) - group * lax.broadcasted_iota(
            jnp.int32, (rows, local), 0
        )
        hit = (off >= 0) & (off < group) & (row > 0.0)
        return jnp.where(hit, 1.0, 0.0), row

    def send_ig(i, zz):
        xx = (x + i) % cols
        return send(
            igs.at[xx, zz], igb.at[xx, zz, c], igs_sem.at[xx, zz], igr_sem.at[xx, zz], x, z, 1 - c
        )

    def send_score(s):
        return pltpu.make_async_remote_copy(
            src_ref=scs.at[s],
            dst_ref=scr.at[me],
            send_sem=scs_sem.at[s],
            recv_sem=scr_sem.at[me],
            device_id={"da": s // depth, "db": s % depth},
            device_id_type=MESH,
        )

    def send_part(o, zz):
        return send(
            ps.at[o, zz],
            pr.at[others - 1 - o, zz],
            ps_sem.at[o, zz],
            pr_sem.at[others - 1 - o, zz],
            (x + 1 + o) % cols,
            z,
            c,
        )

    def send_row(zz):
        return send(rs.at[zz], rz.at[z], rs_sem.at[zz], rz_sem.at[z], x, zz, c)

    blocks = [(i, r) for i in range(cols) for r in range(CORES)]
    batch = len(blocks) * rows

    def compute(j, zz):
        base = pl.multiple_of(j * batch, batch)
        picks = []
        gate_cols = []
        for n, (i, r) in enumerate(blocks):
            s = slot((x + i) % cols, zz, (c + r) % CORES)
            chosen, row = pick(s, me)
            picks.append((s, chosen))
            gate_cols.append(jnp.sum(chosen * row, axis=1, keepdims=True))
            hot = chosen.astype(jnp.bfloat16)
            where = pl.ds(pl.multiple_of(base + n * rows, rows), rows)
            xs[where, :] = dot(hot, tok[s], ((1,), (0,))).astype(jnp.bfloat16)
            su[where, :] = dot(hot, up[s], ((1,), (0,))).astype(jnp.bfloat16)
        here = pl.ds(base, batch)
        gate = jnp.concatenate(gate_cols, axis=0)
        upstream = su[here, :]
        projected = dot(xs[here, :], win[...], ((1,), (0,)))
        back_raw = dot(upstream, wout[...], ((1,), (1,)))
        su[here, :] = (gate * upstream.astype(jnp.float32)).astype(jnp.bfloat16)
        gate_part, up_part = projected[:, :ff], projected[:, ff:]
        activated, derivative = silu_parts(gate_part)
        hidden = (activated * up_part).astype(jnp.bfloat16)
        hid[here, :] = hidden
        scores = jnp.sum(hidden.astype(jnp.float32) * back_raw, axis=1, keepdims=True)
        scores = scores.astype(jnp.bfloat16).astype(jnp.float32)
        back_hidden = gate * back_raw
        gp[here, :ff] = (back_hidden * up_part * derivative).astype(jnp.bfloat16)
        gp[here, ff:] = (back_hidden * activated).astype(jnp.bfloat16)
        grads = dot(gp[here, :], win[...], ((1,), (1,))).astype(jnp.bfloat16)
        for n, (i, r) in enumerate(blocks):
            xx = (x + i) % cols
            piece = grads[n * rows : (n + 1) * rows]
            if r == 0:
                igb[xx, zz, c] = piece
            else:
                igs[xx, zz] = piece
                send_ig(i, zz).start()
        for n, (i, r) in enumerate(blocks):
            s, chosen = picks[n]
            line = jnp.sum(chosen * scores[n * rows : (n + 1) * rows], axis=0, keepdims=True)
            scs[s] = jnp.broadcast_to(line, scs.shape[1:])
            if i == 0 and r == 0:

                @pl.when(zz == z)
                def _():
                    scr[me] = scs[me]

                @pl.when(zz != z)
                def _():
                    send_score(s).start()
            else:
                send_score(s).start()

    def chip_sum(i, zz):
        xx = (x + i) % cols
        s = slot(xx, zz, c)
        hot = jnp.concatenate([pick(s, slot(x, z, k))[0] for k in range(CORES)], axis=0)
        both = igb[xx, zz].reshape(CORES * rows, features)
        return dot(hot.astype(jnp.bfloat16), both, ((0,), (0,)))

    def start(copy):
        copy.start()

    def wait_send(copy):
        copy.wait_send()

    def step(i, carry):
        @pl.when(i < depth)
        def _():
            zz = visit(i, z, depth)

            @pl.when(i > 0)
            def _():
                arrive(slot(x, zz, c))

            spread_column(zz, start)

        @pl.when((i >= 1) & (i <= depth))
        def _():
            j = i - 1
            zz = visit(j, z, depth)
            for o in range(others):
                arrive(slot((x + 1 + o) % cols, zz, c))
                spread_core(o, zz, start)

            @pl.when(i == 1)
            def _():
                loads[2].wait()
                loads[3].wait()

            for k in range(cols):
                arrive(slot((x + k) % cols, zz, 1 - c))
            compute(j, zz)
            for k in list(range(1, cols)) + [0]:
                xx = (x + k) % cols
                send_ig(k, zz).wait_recv()
                total = chip_sum(k, zz)
                if k == 0:
                    pk[zz] = total
                else:
                    ps[k - 1, zz] = total.astype(jnp.bfloat16)
                    send_part(k - 1, zz).start()

        @pl.when(i >= 2)
        def _():
            zz = visit(i - 2, z, depth)
            total = pk[zz]
            for o in range(others):
                send_part(others - 1 - o, zz).wait_recv()
                total = total + pr[o, zz].astype(jnp.float32)

            @pl.when(zz == z)
            def _():
                rk[...] = total

            @pl.when(zz != z)
            def _():
                rs[zz] = total.astype(jnp.bfloat16)
                send_row(zz).start()

        return carry

    lax.fori_loop(0, depth + 2, step, 0)

    wide = min(features, 256)

    @pl.loop(0, features // wide)
    def _(t):
        at = pl.ds(pl.multiple_of(t * wide, wide), wide)
        gin_ref[0, at, :] = dot(xs[:, at], gp[...], ((0,), (0,))).astype(jnp.bfloat16)

    thin = 128

    @pl.loop(0, ff // thin)
    def _(t):
        at = pl.ds(pl.multiple_of(t * thin, thin), thin)
        gdown_ref[0, at, :] = dot(hid[:, at], su[...], ((0,), (0,))).astype(jnp.bfloat16)

    @pl.loop(1, count)
    def _(k):
        s = (me + k) % count
        pltpu.make_async_remote_copy(
            src_ref=scs.at[s],
            dst_ref=scr.at[s],
            send_sem=scs_sem.at[s],
            recv_sem=scr_sem.at[s],
            device_id={"da": s // depth, "db": s % depth},
            device_id_type=MESH,
        ).wait()

    lines = scr[:, 0, :]
    pad = jnp.zeros((local - experts, local), jnp.float32)
    scores = jnp.concatenate([lines, pad], axis=0).T if experts < local else lines.T
    place = lax.broadcasted_iota(jnp.int32, (local, top), 1)
    gate_grads = jnp.zeros((local, top), jnp.float32)
    for k in range(top):
        value = jnp.sum(jnp.where(routes[:, k : k + 1] == lanes, scores, 0.0), axis=1, keepdims=True)
        gate_grads = jnp.where(place == k, value, gate_grads)
    gg_ref[...] = gate_grads.astype(jnp.bfloat16)

    def finish(k, carry):
        zz = (z + k) % depth
        send(rs.at[zz], rz.at[zz], rs_sem.at[zz], rz_sem.at[zz], x, zz, c).wait()
        rk[...] += rz[zz].astype(jnp.float32)
        return carry

    lax.fori_loop(1, depth, finish, 0)
    tg_ref[...] = rk[...].astype(jnp.bfloat16)

    def drain(zz, carry):
        spread_column(zz, wait_send)
        for o in range(others):
            spread_core(o, zz, wait_send)
            send_part(o, zz).wait_send()
        for k in range(cols):
            send_ig(k, zz).wait_send()
        return carry

    lax.fori_loop(0, depth, drain, 0)


def fused(tokens, grad_out, routes, gates, w_gate_up, w_down):
    first_size, depth = lax.axis_size("da"), lax.axis_size("db")
    cols = first_size // CORES
    experts = first_size * depth
    local, features = tokens.shape
    top = routes.shape[1]
    group = experts // top
    rows = local // group
    ff = w_down.shape[1]
    bf, f32 = jnp.bfloat16, jnp.float32
    total = rows * experts
    dma = pltpu.SemaphoreType.DMA
    scratch = [
        pltpu.VMEM((experts, local, features), bf),
        pltpu.VMEM((experts, local, features), bf),
        pltpu.VMEM((experts, experts, local), bf),
        pltpu.VMEM((features, 2 * ff), bf),
        pltpu.VMEM((ff, features), bf),
        pltpu.VMEM((total, features), bf),
        pltpu.VMEM((total, features), bf),
        pltpu.VMEM((total, ff), bf),
        pltpu.VMEM((total, 2 * ff), bf),
        pltpu.VMEM((cols, depth, rows, features), bf),
        pltpu.VMEM((cols, depth, CORES, rows, features), bf),
        pltpu.VMEM((cols - 1, depth, local, features), bf),
        pltpu.VMEM((depth, local, features), f32),
        pltpu.VMEM((cols - 1, depth, local, features), bf),
        pltpu.VMEM((depth, local, features), bf),
        pltpu.VMEM((local, features), f32),
        pltpu.VMEM((depth, local, features), bf),
        pltpu.VMEM((experts, 8, local), f32),
        pltpu.VMEM((experts, 8, local), f32),
        dma((4,)),
        dma((experts, 3)),
        dma((depth, 3)),
        dma((depth, 3)),
        dma((cols - 1, depth, 3)),
        dma((cols, depth, 3)),
        dma((cols, depth)),
        dma((cols, depth)),
        dma((cols - 1, depth)),
        dma((cols - 1, depth)),
        dma((depth,)),
        dma((depth,)),
        dma((experts,)),
        dma((experts,)),
    ]
    vmem = pl.BlockSpec(memory_space=pltpu.VMEM)
    hbm = pl.BlockSpec(memory_space=pl.ANY)
    return pl.pallas_call(
        functools.partial(fused_kernel, cols, depth, group),
        out_shape=(
            jax.ShapeDtypeStruct((local, features), bf),
            jax.ShapeDtypeStruct((local, top), bf),
            jax.ShapeDtypeStruct(w_gate_up.shape, bf),
            jax.ShapeDtypeStruct(w_down.shape, bf),
        ),
        in_specs=[hbm, hbm, vmem, vmem, hbm, hbm],
        out_specs=(vmem, vmem, vmem, vmem),
        scratch_shapes=scratch,
        compiler_params=pltpu.CompilerParams(
            collective_id=0, has_side_effects=True, vmem_limit_bytes=60 * 2**20
        ),
    )(tokens, grad_out, routes, gates, w_gate_up, w_down)


def fits(tokens, routes, w_down):
    first_size = lax.axis_size("da")
    experts = first_size * lax.axis_size("db")
    local, features = tokens.shape
    group = experts // routes.shape[1]
    held = 2 * experts * local * features * 2
    return (
        lax.axis_size("replica") == 1
        and first_size % CORES == 0
        and first_size > CORES
        and held <= 16 * 2**20
        and local == 128
        and experts <= local
        and (local // group) % 16 == 0
        and w_down.shape[1] % 128 == 0
    )


def route(*arrays):
    if fits(arrays[0], arrays[2], arrays[5]):
        return fused(*arrays)
    return body(*arrays)


def solution(mesh):
    placed = (
        P(("groups", "replica", "da", "db"), None),
        P(("groups", "replica", "da", "db"), None),
        P(("groups", "replica", "da", "db"), None),
        P(("groups", "replica", "da", "db"), None),
        P(("da", "db"), "replica", None),
        P(("da", "db"), "replica", None),
    )
    return jax.shard_map(
        route,
        mesh=mesh,
        in_specs=placed,
        out_specs=(
            P(("groups", "replica", "da", "db"), None),
            P(("groups", "replica", "da", "db"), None),
            P(("groups", "da", "db"), "replica", None),
            P(("groups", "da", "db"), "replica", None),
        ),
        check_vma=False,
    )
```

```python
import functools

import jax
import jax.numpy as jnp
from jax import lax
from jax.experimental import pallas as pl
from jax.experimental.pallas import tpu as pltpu
from jax.sharding import PartitionSpec as P


CORES = 2
MESH = pl.DeviceIdType.MESH


def silu_parts(projected):
    sigmoid = jax.nn.sigmoid(projected)
    return (projected * sigmoid, sigmoid * (1.0 + projected * (1.0 - sigmoid)))


def body(tokens, grad_out, routes, gates, w_gate_up, w_down):
    local_tokens, features = tokens.shape
    top_count = routes.shape[1]
    hidden_units = w_gate_up.shape[2] // 2
    first_size = lax.axis_size("da")
    second_size = lax.axis_size("db")
    experts = first_size * second_size
    per_round = experts // top_count
    rounds = local_tokens // per_round
    expert_ids = lax.broadcasted_iota(jnp.int32, (1, 1, 1, experts), 3)
    matches = routes.reshape(rounds, per_round, top_count, 1) == expert_ids
    gate_values = gates.reshape(rounds, per_round, top_count, 1).astype(jnp.float32)
    gate_table = jnp.sum(jnp.where(matches, gate_values, 0.0), axis=(1, 2)).astype(jnp.bfloat16)
    chosen = jnp.any(matches, axis=2).astype(jnp.bfloat16)
    input_send = jnp.einsum(
        "rge,rgd->red",
        chosen,
        tokens.reshape(rounds, per_round, features),
        preferred_element_type=jnp.float32,
    ).astype(jnp.bfloat16)
    upstream_send = jnp.einsum(
        "rge,rgd->red",
        chosen,
        grad_out.reshape(rounds, per_round, features),
        preferred_element_type=jnp.float32,
    ).astype(jnp.bfloat16)
    input_recv, upstream_recv, gate_recv = (
        lax.all_to_all(input_send, ("da", "db"), split_axis=1, concat_axis=1, tiled=True),
        lax.all_to_all(upstream_send, ("da", "db"), split_axis=1, concat_axis=1, tiled=True),
        lax.all_to_all(gate_table, ("da", "db"), split_axis=1, concat_axis=1, tiled=True),
    )
    input_rows = input_recv.reshape(-1, features)
    upstream_rows = upstream_recv.reshape(-1, features)
    gate_rows = gate_recv.reshape(-1, 1).astype(jnp.float32)
    w_in, w_out = (
        lax.all_gather(w_gate_up[0], "replica", axis=0, tiled=True),
        lax.all_gather(w_down[0], "replica", axis=0, tiled=True),
    )
    projected = jnp.dot(input_rows, w_in, preferred_element_type=jnp.float32)
    back_raw = jnp.einsum("rd,fd->rf", upstream_rows, w_out, preferred_element_type=jnp.float32)
    gate_part = projected[:, :hidden_units]
    up_part = projected[:, hidden_units:]
    activated, derivative = silu_parts(gate_part)
    hidden = (activated * up_part).astype(jnp.bfloat16)
    gate_scores = jnp.sum(hidden.astype(jnp.float32) * back_raw, axis=1).astype(jnp.bfloat16)
    back_hidden = gate_rows * back_raw
    grad_projected = jnp.concatenate(
        [back_hidden * up_part * derivative, back_hidden * activated], axis=1
    ).astype(jnp.bfloat16)
    scaled_upstream = (gate_rows * upstream_rows.astype(jnp.float32)).astype(jnp.bfloat16)
    input_grads = jnp.einsum("rf,df->rd", grad_projected, w_in, preferred_element_type=jnp.float32)
    input_grads = input_grads.astype(jnp.bfloat16).reshape(rounds, experts, features)
    score_back = gate_scores.reshape(rounds, experts)
    returned, score_ret = (
        lax.all_to_all(input_grads, ("da", "db"), split_axis=1, concat_axis=1, tiled=True),
        lax.all_to_all(score_back, ("da", "db"), split_axis=1, concat_axis=1, tiled=True),
    )
    score_ret = score_ret.reshape(rounds, 1, 1, experts).astype(jnp.float32)
    token_grads = (
        jnp.einsum("rge,red->rgd", chosen, returned, preferred_element_type=jnp.float32)
        .astype(jnp.bfloat16)
        .reshape(local_tokens, features)
    )
    gate_grads = (
        jnp.sum(jnp.where(matches, score_ret, 0.0), axis=3)
        .astype(jnp.bfloat16)
        .reshape(local_tokens, top_count)
    )
    columns = input_rows
    grad_in = lax.psum_scatter(
        jnp.einsum("rd,rf->df", columns, grad_projected, preferred_element_type=jnp.float32).astype(
            jnp.bfloat16
        ),
        "replica",
        scatter_dimension=0,
        tiled=True,
    )
    columns = hidden
    grad_down = lax.psum_scatter(
        jnp.einsum(
            "rf,rd->fd", columns, scaled_upstream, preferred_element_type=jnp.float32
        ).astype(jnp.bfloat16),
        "replica",
        scatter_dimension=0,
        tiled=True,
    )
    return (token_grads, gate_grads, grad_in[None], grad_down[None])


def visit(j, z, n):
    m = jnp.minimum(z, n - 1 - z)
    near = z + (1 - 2 * (j % 2)) * ((j + 1) // 2)
    far = jnp.where(z < n - 1 - z, j, n - 1 - j)
    return jnp.where(j <= 2 * m, near, far)


def dot(a, b, dims):
    return lax.dot_general(a, b, (dims, ((), ())), preferred_element_type=jnp.float32)


def fused_kernel(
    cols, depth, group,
    tok_hbm, up_hbm, routes_ref, gates_ref, win_hbm, wout_hbm,
    tg_ref, gg_ref, gin_ref, gdown_ref,
    tok, up, table, win, wout, xs, su, hid, gp, igs, igb, ps, pk, pr, rs, rk, rz, scs, scr,
    load_sem, recv_sem, zup_sem, zdn_sem, x_sem, o_sem, p_sem, igs_sem, igr_sem, ps_sem, pr_sem, rs_sem, rz_sem,
    scs_sem, scr_sem,
):
    da = lax.axis_index("da")
    z = lax.axis_index("db")
    x, c = da // CORES, da % CORES
    local, features = tok.shape[1], tok.shape[2]
    experts = table.shape[1]
    top = routes_ref.shape[0]
    rows = local // group
    ff = wout.shape[0]
    others = cols - 1

    def slot(xx, zz, cc):
        return (xx * CORES + cc) * depth + zz

    me = slot(x, z, c)
    loads = [
        pltpu.make_async_copy(tok_hbm, tok.at[me], load_sem.at[0]),
        pltpu.make_async_copy(up_hbm, up.at[me], load_sem.at[1]),
        pltpu.make_async_copy(win_hbm.at[0], win, load_sem.at[2]),
        pltpu.make_async_copy(wout_hbm.at[0], wout, load_sem.at[3]),
    ]
    for one in loads:
        one.start()

    barrier = pltpu.get_barrier_semaphore()
    count = cols * CORES * depth

    @pl.loop(1, count)
    def _(k):
        to = (me + k) % count
        pl.semaphore_signal(
            barrier, inc=1, device_id={"da": to // depth, "db": to % depth}, device_id_type=MESH
        )

    routes = routes_ref[...]
    gates = gates_ref[...].astype(jnp.float32)
    ids = lax.broadcasted_iota(jnp.int32, (experts, local), 0)
    chart = jnp.zeros((experts, local), jnp.float32)
    for k in range(top):
        chart = chart + jnp.where(routes[k : k + 1] == ids, gates[k : k + 1], 0.0)
    table[me] = chart.astype(jnp.bfloat16)

    pl.semaphore_wait(barrier, count - 1)
    loads[0].wait()
    loads[1].wait()

    held = (table, tok, up)

    def send(src, dst, send_sem, recv, to_x, to_z, to_c):
        return pltpu.make_async_remote_copy(
            src_ref=src,
            dst_ref=dst,
            send_sem=send_sem,
            recv_sem=recv,
            device_id={"da": to_x * CORES + to_c, "db": to_z},
            device_id_type=MESH,
        )

    def relay(s, a, sem, to_x, to_z, to_c):
        ref = held[a].at[s]
        return send(ref, ref, sem, recv_sem.at[s, a], to_x, to_z, to_c)

    def arrive(s):
        for a in range(3):
            relay(s, a, p_sem.at[0, 0, a], x, z, 1 - c).wait_recv()

    def along(row, zz, a):
        last = depth - 1
        near = ((row == 1) & (zz == 0)) | ((row == last - 1) & (zz == last))
        if a != 2:
            return near
        return near | ((row == 0) & (zz == last)) | ((row == last) & (zz == 0))

    def spread_column(zz, act):
        s = slot(x, zz, c)

        @pl.when((zz <= z) & (z < depth - 1))
        def _():
            for a in range(3):
                act(relay(s, a, zup_sem.at[zz, a], x, z + 1, c))

        @pl.when((zz >= z) & (z > 0))
        def _():
            for a in range(3):
                act(relay(s, a, zdn_sem.at[zz, a], x, z - 1, c))

        for a in range(3):
            for o in range(others):

                @pl.when(jnp.logical_not(along(z, zz, a)))
                def _():
                    act(relay(s, a, x_sem.at[o, zz, a], (x + 1 + o) % cols, z, c))
        for a in range(3):
            act(relay(s, a, p_sem.at[0, zz, a], x, z, 1 - c))

    def spread_core(o, zz, act):
        s = slot((x + 1 + o) % cols, zz, c)
        last = depth - 1
        for a in range(3):
            up = ((z == 0) & along(1, zz, a)) | ((z == last - 1) & along(last, zz, a) & (zz == 0))
            down = ((z == last) & along(last - 1, zz, a)) | ((z == 1) & along(0, zz, a) & (zz == last))
            up = up & jnp.logical_not((z == 0) & (zz != 0))
            down = down & jnp.logical_not((z == last) & (zz != last))

            @pl.when(up)
            def _():
                act(relay(s, a, o_sem.at[o, zz, a], x, z + 1, c))

            @pl.when(down)
            def _():
                act(relay(s, a, o_sem.at[o, zz, a], x, z - 1, c))

        for a in range(3):
            act(relay(s, a, p_sem.at[1 + o, zz, a], x, z, 1 - c))

    def pick(s, e):
        chart_s = table[s].astype(jnp.float32)
        which = lax.broadcasted_iota(jnp.int32, chart_s.shape, 0) == e
        row = jnp.sum(jnp.where(which, chart_s, 0.0), axis=0, keepdims=True)
        off = lax.broadcasted_iota(jnp.int32, (rows, local), 1) - group * lax.broadcasted_iota(
            jnp.int32, (rows, local), 0
        )
        hit = (off >= 0) & (off < group) & (row > 0.0)
        return jnp.where(hit, 1.0, 0.0), row

    def send_ig(i, zz):
        xx = (x + i) % cols
        return send(
            igs.at[xx, zz], igb.at[xx, zz, c], igs_sem.at[xx, zz], igr_sem.at[xx, zz], x, z, 1 - c
        )

    def send_score(s):
        return pltpu.make_async_remote_copy(
            src_ref=scs.at[s],
            dst_ref=scr.at[me],
            send_sem=scs_sem.at[s],
            recv_sem=scr_sem.at[me],
            device_id={"da": s // depth, "db": s % depth},
            device_id_type=MESH,
        )

    def send_part(o, zz):
        return send(
            ps.at[o, zz],
            pr.at[others - 1 - o, zz],
            ps_sem.at[o, zz],
            pr_sem.at[others - 1 - o, zz],
            (x + 1 + o) % cols,
            z,
            c,
        )

    def send_row(zz):
        return send(rs.at[zz], rz.at[z], rs_sem.at[zz], rz_sem.at[z], x, zz, c)

    blocks = [(i, r) for i in range(cols) for r in range(CORES)]
    batch = len(blocks) * rows

    def compute(j, zz):
        base = pl.multiple_of(j * batch, batch)
        picks = []
        gate_cols = []
        for n, (i, r) in enumerate(blocks):
            s = slot((x + i) % cols, zz, (c + r) % CORES)
            chosen, row = pick(s, me)
            picks.append((s, chosen))
            gate_cols.append(jnp.sum(chosen * row, axis=1, keepdims=True))
            hot = chosen.astype(jnp.bfloat16)
            where = pl.ds(pl.multiple_of(base + n * rows, rows), rows)
            xs[where, :] = dot(hot, tok[s], ((1,), (0,))).astype(jnp.bfloat16)
            su[where, :] = dot(hot, up[s], ((1,), (0,))).astype(jnp.bfloat16)
        here = pl.ds(base, batch)
        gate = jnp.concatenate(gate_cols, axis=0)
        upstream = su[here, :]
        projected = dot(xs[here, :], win[...], ((1,), (0,)))
        back_raw = dot(upstream, wout[...], ((1,), (1,)))
        su[here, :] = (gate * upstream.astype(jnp.float32)).astype(jnp.bfloat16)
        gate_part, up_part = projected[:, :ff], projected[:, ff:]
        activated, derivative = silu_parts(gate_part)
        hidden = (activated * up_part).astype(jnp.bfloat16)
        hid[here, :] = hidden
        scores = jnp.sum(hidden.astype(jnp.float32) * back_raw, axis=1, keepdims=True)
        scores = scores.astype(jnp.bfloat16).astype(jnp.float32)
        back_hidden = gate * back_raw
        gp[here, :ff] = (back_hidden * up_part * derivative).astype(jnp.bfloat16)
        gp[here, ff:] = (back_hidden * activated).astype(jnp.bfloat16)
        grads = dot(gp[here, :], win[...], ((1,), (1,))).astype(jnp.bfloat16)
        for n, (i, r) in enumerate(blocks):
            xx = (x + i) % cols
            piece = grads[n * rows : (n + 1) * rows]
            if r == 0:
                igb[xx, zz, c] = piece
            else:
                igs[xx, zz] = piece
                send_ig(i, zz).start()
        for n, (i, r) in enumerate(blocks):
            s, chosen = picks[n]
            line = jnp.sum(chosen * scores[n * rows : (n + 1) * rows], axis=0, keepdims=True)
            scs[s] = jnp.broadcast_to(line, scs.shape[1:])
            if i == 0 and r == 0:

                @pl.when(zz == z)
                def _():
                    scr[me] = scs[me]

                @pl.when(zz != z)
                def _():
                    send_score(s).start()
            else:
                send_score(s).start()

    def chip_sum(i, zz):
        xx = (x + i) % cols
        s = slot(xx, zz, c)
        hot = jnp.concatenate([pick(s, slot(x, z, k))[0] for k in range(CORES)], axis=0)
        both = igb[xx, zz].reshape(CORES * rows, features)
        return dot(hot.astype(jnp.bfloat16), both, ((0,), (0,)))

    def start(copy):
        copy.start()

    def wait_send(copy):
        copy.wait_send()

    def step(i, carry):
        @pl.when(i < depth)
        def _():
            zz = visit(i, z, depth)

            @pl.when(i > 0)
            def _():
                arrive(slot(x, zz, c))

            spread_column(zz, start)

        @pl.when((i >= 2) & (i < depth + 2))
        def _():
            j = i - 2
            zz = visit(j, z, depth)

            @pl.when(j == 0)
            def _():
                loads[2].wait()
                loads[3].wait()

            for k in range(cols):
                arrive(slot((x + k) % cols, zz, 1 - c))
            compute(j, zz)
            for k in list(range(1, cols)) + [0]:
                send_ig(k, zz).wait_recv()
                total = chip_sum(k, zz)
                if k == 0:
                    pk[zz] = total
                else:
                    ps[k - 1, zz] = total.astype(jnp.bfloat16)
                    send_part(k - 1, zz).start()

        @pl.when((i >= 1) & (i <= depth))
        def _():
            zz = visit(i - 1, z, depth)
            for o in range(others):
                arrive(slot((x + 1 + o) % cols, zz, c))
                spread_core(o, zz, start)

        @pl.when(i >= 4)
        def _():
            zz = visit(i - 4, z, depth)
            total = pk[zz]
            for o in range(others):
                send_part(others - 1 - o, zz).wait_recv()
                total = total + pr[o, zz].astype(jnp.float32)

            @pl.when(zz == z)
            def _():
                rk[...] = total

            @pl.when(zz != z)
            def _():
                rs[zz] = total.astype(jnp.bfloat16)
                send_row(zz).start()

        return carry

    lax.fori_loop(0, depth + 4, step, 0)

    wide = min(features, 256)

    @pl.loop(0, features // wide)
    def _(t):
        at = pl.ds(pl.multiple_of(t * wide, wide), wide)
        gin_ref[0, at, :] = dot(xs[:, at], gp[...], ((0,), (0,))).astype(jnp.bfloat16)

    thin = 128

    @pl.loop(0, ff // thin)
    def _(t):
        at = pl.ds(pl.multiple_of(t * thin, thin), thin)
        gdown_ref[0, at, :] = dot(hid[:, at], su[...], ((0,), (0,))).astype(jnp.bfloat16)

    @pl.loop(1, count)
    def _(k):
        s = (me + k) % count
        pltpu.make_async_remote_copy(
            src_ref=scs.at[s],
            dst_ref=scr.at[s],
            send_sem=scs_sem.at[s],
            recv_sem=scr_sem.at[s],
            device_id={"da": s // depth, "db": s % depth},
            device_id_type=MESH,
        ).wait()

    scores = scr[:, 0, :]
    place = lax.broadcasted_iota(jnp.int32, (top, local), 0)
    gate_grads = jnp.zeros((top, local), jnp.float32)
    for k in range(top):
        value = jnp.sum(jnp.where(routes[k : k + 1] == ids, scores, 0.0), axis=0, keepdims=True)
        gate_grads = jnp.where(place == k, value, gate_grads)
    gg_ref[...] = gate_grads.astype(jnp.bfloat16)

    def finish(k, carry):
        zz = (z + k) % depth
        send(rs.at[zz], rz.at[zz], rs_sem.at[zz], rz_sem.at[zz], x, zz, c).wait()
        rk[...] += rz[zz].astype(jnp.float32)
        return carry

    lax.fori_loop(1, depth, finish, 0)
    tg_ref[...] = rk[...].astype(jnp.bfloat16)

    def drain(zz, carry):
        spread_column(zz, wait_send)
        for o in range(others):
            spread_core(o, zz, wait_send)
            send_part(o, zz).wait_send()
        for k in range(cols):
            send_ig(k, zz).wait_send()
        return carry

    lax.fori_loop(0, depth, drain, 0)


def fused(tokens, grad_out, routes, gates, w_gate_up, w_down):
    first_size, depth = lax.axis_size("da"), lax.axis_size("db")
    cols = first_size // CORES
    experts = first_size * depth
    local, features = tokens.shape
    top = routes.shape[1]
    group = experts // top
    rows = local // group
    ff = w_down.shape[1]
    bf, f32 = jnp.bfloat16, jnp.float32
    total = rows * experts
    dma = pltpu.SemaphoreType.DMA
    scratch = [
        pltpu.VMEM((experts, local, features), bf),
        pltpu.VMEM((experts, local, features), bf),
        pltpu.VMEM((experts, experts, local), bf),
        pltpu.VMEM((features, 2 * ff), bf),
        pltpu.VMEM((ff, features), bf),
        pltpu.VMEM((total, features), bf),
        pltpu.VMEM((total, features), bf),
        pltpu.VMEM((total, ff), bf),
        pltpu.VMEM((total, 2 * ff), bf),
        pltpu.VMEM((cols, depth, rows, features), bf),
        pltpu.VMEM((cols, depth, CORES, rows, features), bf),
        pltpu.VMEM((cols - 1, depth, local, features), bf),
        pltpu.VMEM((depth, local, features), f32),
        pltpu.VMEM((cols - 1, depth, local, features), bf),
        pltpu.VMEM((depth, local, features), bf),
        pltpu.VMEM((local, features), f32),
        pltpu.VMEM((depth, local, features), bf),
        pltpu.VMEM((experts, 8, local), f32),
        pltpu.VMEM((experts, 8, local), f32),
        dma((4,)),
        dma((experts, 3)),
        dma((depth, 3)),
        dma((depth, 3)),
        dma((cols - 1, depth, 3)),
        dma((cols - 1, depth, 3)),
        dma((cols, depth, 3)),
        dma((cols, depth)),
        dma((cols, depth)),
        dma((cols - 1, depth)),
        dma((cols - 1, depth)),
        dma((depth,)),
        dma((depth,)),
        dma((experts,)),
        dma((experts,)),
    ]
    vmem = pl.BlockSpec(memory_space=pltpu.VMEM)
    hbm = pl.BlockSpec(memory_space=pltpu.HBM)
    token_grads, gate_grads, grad_in, grad_down = pl.pallas_call(
        functools.partial(fused_kernel, cols, depth, group),
        out_shape=(
            jax.ShapeDtypeStruct((local, features), bf),
            jax.ShapeDtypeStruct((top, local), bf),
            jax.ShapeDtypeStruct(w_gate_up.shape, bf),
            jax.ShapeDtypeStruct(w_down.shape, bf),
        ),
        in_specs=[hbm, hbm, vmem, vmem, hbm, hbm],
        out_specs=(vmem, vmem, vmem, vmem),
        scratch_shapes=scratch,
        compiler_params=pltpu.CompilerParams(
            collective_id=0, has_side_effects=True, vmem_limit_bytes=44 * 2**20
        ),
    )(*(pltpu.with_memory_space_constraint(a, pltpu.HBM) for a in (tokens, grad_out)), routes.T, gates.T,
      *(pltpu.with_memory_space_constraint(a, pltpu.HBM) for a in (w_gate_up, w_down)))
    return token_grads, gate_grads.T, grad_in, grad_down


def fits(tokens, routes, w_down):
    first_size = lax.axis_size("da")
    experts = first_size * lax.axis_size("db")
    local, features = tokens.shape
    group = experts // routes.shape[1]
    held = 2 * experts * local * features * 2
    return (
        lax.axis_size("replica") == 1
        and first_size % CORES == 0
        and first_size > CORES
        and lax.axis_size("db") >= 4
        and held <= 16 * 2**20
        and local == 128
        and experts <= local
        and (local // group) % 16 == 0
        and w_down.shape[1] % 128 == 0
    )


def route(*arrays):
    if fits(arrays[0], arrays[2], arrays[5]):
        return fused(*arrays)
    return body(*arrays)


def solution(mesh):
    placed = (
        P(("groups", "replica", "da", "db"), None),
        P(("groups", "replica", "da", "db"), None),
        P(("groups", "replica", "da", "db"), None),
        P(("groups", "replica", "da", "db"), None),
        P(("da", "db"), "replica", None),
        P(("da", "db"), "replica", None),
    )
    return jax.shard_map(
        route,
        mesh=mesh,
        in_specs=placed,
        out_specs=(
            P(("groups", "replica", "da", "db"), None),
            P(("groups", "replica", "da", "db"), None),
            P(("groups", "da", "db"), "replica", None),
            P(("groups", "da", "db"), "replica", None),
        ),
        check_vma=False,
    )
```

```python
import functools

import jax
import jax.numpy as jnp
from jax import lax
from jax.experimental import pallas as pl
from jax.experimental.pallas import tpu as pltpu
from jax.sharding import PartitionSpec as P


CORES = 2
PIECES = 4
MESH = pl.DeviceIdType.MESH


def silu_parts(projected):
    sigmoid = jax.nn.sigmoid(projected)
    return (projected * sigmoid, sigmoid * (1.0 + projected * (1.0 - sigmoid)))


def body(tokens, grad_out, routes, gates, w_gate_up, w_down):
    local_tokens, features = tokens.shape
    top_count = routes.shape[1]
    hidden_units = w_gate_up.shape[2] // 2
    first_size = lax.axis_size("da")
    second_size = lax.axis_size("db")
    experts = first_size * second_size
    per_round = experts // top_count
    rounds = local_tokens // per_round
    expert_ids = lax.broadcasted_iota(jnp.int32, (1, 1, 1, experts), 3)
    matches = routes.reshape(rounds, per_round, top_count, 1) == expert_ids
    gate_values = gates.reshape(rounds, per_round, top_count, 1).astype(jnp.float32)
    gate_table = jnp.sum(jnp.where(matches, gate_values, 0.0), axis=(1, 2)).astype(jnp.bfloat16)
    chosen = jnp.any(matches, axis=2).astype(jnp.bfloat16)
    input_send = jnp.einsum(
        "rge,rgd->red",
        chosen,
        tokens.reshape(rounds, per_round, features),
        preferred_element_type=jnp.float32,
    ).astype(jnp.bfloat16)
    upstream_send = jnp.einsum(
        "rge,rgd->red",
        chosen,
        grad_out.reshape(rounds, per_round, features),
        preferred_element_type=jnp.float32,
    ).astype(jnp.bfloat16)
    input_recv, upstream_recv, gate_recv = (
        lax.all_to_all(input_send, ("da", "db"), split_axis=1, concat_axis=1, tiled=True),
        lax.all_to_all(upstream_send, ("da", "db"), split_axis=1, concat_axis=1, tiled=True),
        lax.all_to_all(gate_table, ("da", "db"), split_axis=1, concat_axis=1, tiled=True),
    )
    input_rows = input_recv.reshape(-1, features)
    upstream_rows = upstream_recv.reshape(-1, features)
    gate_rows = gate_recv.reshape(-1, 1).astype(jnp.float32)
    w_in, w_out = (
        lax.all_gather(w_gate_up[0], "replica", axis=0, tiled=True),
        lax.all_gather(w_down[0], "replica", axis=0, tiled=True),
    )
    projected = jnp.dot(input_rows, w_in, preferred_element_type=jnp.float32)
    back_raw = jnp.einsum("rd,fd->rf", upstream_rows, w_out, preferred_element_type=jnp.float32)
    gate_part = projected[:, :hidden_units]
    up_part = projected[:, hidden_units:]
    activated, derivative = silu_parts(gate_part)
    hidden = (activated * up_part).astype(jnp.bfloat16)
    gate_scores = jnp.sum(hidden.astype(jnp.float32) * back_raw, axis=1).astype(jnp.bfloat16)
    back_hidden = gate_rows * back_raw
    grad_projected = jnp.concatenate(
        [back_hidden * up_part * derivative, back_hidden * activated], axis=1
    ).astype(jnp.bfloat16)
    scaled_upstream = (gate_rows * upstream_rows.astype(jnp.float32)).astype(jnp.bfloat16)
    input_grads = jnp.einsum("rf,df->rd", grad_projected, w_in, preferred_element_type=jnp.float32)
    input_grads = input_grads.astype(jnp.bfloat16).reshape(rounds, experts, features)
    score_back = gate_scores.reshape(rounds, experts)
    returned, score_ret = (
        lax.all_to_all(input_grads, ("da", "db"), split_axis=1, concat_axis=1, tiled=True),
        lax.all_to_all(score_back, ("da", "db"), split_axis=1, concat_axis=1, tiled=True),
    )
    score_ret = score_ret.reshape(rounds, 1, 1, experts).astype(jnp.float32)
    token_grads = (
        jnp.einsum("rge,red->rgd", chosen, returned, preferred_element_type=jnp.float32)
        .astype(jnp.bfloat16)
        .reshape(local_tokens, features)
    )
    gate_grads = (
        jnp.sum(jnp.where(matches, score_ret, 0.0), axis=3)
        .astype(jnp.bfloat16)
        .reshape(local_tokens, top_count)
    )
    columns = input_rows
    grad_in = lax.psum_scatter(
        jnp.einsum("rd,rf->df", columns, grad_projected, preferred_element_type=jnp.float32).astype(
            jnp.bfloat16
        ),
        "replica",
        scatter_dimension=0,
        tiled=True,
    )
    columns = hidden
    grad_down = lax.psum_scatter(
        jnp.einsum(
            "rf,rd->fd", columns, scaled_upstream, preferred_element_type=jnp.float32
        ).astype(jnp.bfloat16),
        "replica",
        scatter_dimension=0,
        tiled=True,
    )
    return (token_grads, gate_grads, grad_in[None], grad_down[None])


def visit(j, z, n):
    m = jnp.minimum(z, n - 1 - z)
    near = z + (1 - 2 * (j % 2)) * ((j + 1) // 2)
    far = jnp.where(z < n - 1 - z, j, n - 1 - j)
    return jnp.where(j <= 2 * m, near, far)


def dot(a, b, dims):
    return lax.dot_general(a, b, (dims, ((), ())), preferred_element_type=jnp.float32)


def fused_kernel(
    cols, depth, group,
    tok_hbm, up_hbm, routes_hbm, gates_hbm, win_hbm, wout_hbm,
    tg_ref, gg_ref, gin_ref, gdown_ref,
    routes_ref, gates_ref, tok, up, table, win, wout, xs, su, hid, gp, igs, igb, ps, pk, pr, rs, rk, rz, scs, scr,
    load_sem, recv_sem, zup_sem, zdn_sem, x_sem, o_sem, p_sem, igs_sem, igr_sem, ps_sem, pr_sem, rs_sem, rz_sem,
    scs_sem, scr_sem,
):
    da = lax.axis_index("da")
    z = lax.axis_index("db")
    x, c = da // CORES, da % CORES
    local, features = tok.shape[1], tok.shape[2]
    experts = table.shape[1]
    top = routes_ref.shape[0]
    rows = local // group
    ff = wout.shape[0]
    others = cols - 1

    def slot(xx, zz, cc):
        return (xx * CORES + cc) * depth + zz

    me = slot(x, z, c)
    loads = [
        pltpu.make_async_copy(tok_hbm, tok.at[me], load_sem.at[0]),
        pltpu.make_async_copy(up_hbm, up.at[me], load_sem.at[1]),
        pltpu.make_async_copy(win_hbm.at[0], win, load_sem.at[2]),
        pltpu.make_async_copy(wout_hbm.at[0], wout, load_sem.at[3]),
        pltpu.make_async_copy(routes_hbm, routes_ref, load_sem.at[4]),
        pltpu.make_async_copy(gates_hbm, gates_ref, load_sem.at[5]),
    ]
    for k in (4, 5, 0, 1, 2, 3):
        loads[k].start()

    barrier = pltpu.get_barrier_semaphore()
    count = cols * CORES * depth

    @pl.loop(1, count)
    def _(k):
        to = (me + k) % count
        pl.semaphore_signal(
            barrier, inc=1, device_id={"da": to // depth, "db": to % depth}, device_id_type=MESH
        )

    loads[4].wait()
    loads[5].wait()
    routes = routes_ref[...]
    gates = gates_ref[...].astype(jnp.float32)
    ids = lax.broadcasted_iota(jnp.int32, (experts, local), 0)
    chart = jnp.zeros((experts, local), jnp.float32)
    for k in range(top):
        chart = chart + jnp.where(routes[k : k + 1] == ids, gates[k : k + 1], 0.0)
    table[me] = chart.astype(jnp.bfloat16)

    pl.semaphore_wait(barrier, count - 1)
    loads[0].wait()
    loads[1].wait()

    held = (table, tok, up)

    def send(src, dst, send_sem, recv, to_x, to_z, to_c):
        return pltpu.make_async_remote_copy(
            src_ref=src,
            dst_ref=dst,
            send_sem=send_sem,
            recv_sem=recv,
            device_id={"da": to_x * CORES + to_c, "db": to_z},
            device_id_type=MESH,
        )

    def relay(s, a, sem, to_x, to_z, to_c):
        ref = held[a].at[s]
        return send(ref, ref, sem, recv_sem.at[s, a], to_x, to_z, to_c)

    def arrive(s):
        for a in range(3):
            relay(s, a, p_sem.at[0, 0, a], x, z, 1 - c).wait_recv()

    def along(row, zz, a):
        last = depth - 1
        near = ((row == 1) & (zz == 0)) | ((row == last - 1) & (zz == last))
        if a != 2:
            return near
        return near | ((row == 0) & (zz == last)) | ((row == last) & (zz == 0))

    def spread_column(zz, act):
        s = slot(x, zz, c)

        @pl.when((zz <= z) & (z < depth - 1))
        def _():
            for a in range(3):
                act(relay(s, a, zup_sem.at[zz, a], x, z + 1, c))

        @pl.when((zz >= z) & (z > 0))
        def _():
            for a in range(3):
                act(relay(s, a, zdn_sem.at[zz, a], x, z - 1, c))

        for a in range(3):
            for o in range(others):

                @pl.when(jnp.logical_not(along(z, zz, a)))
                def _():
                    act(relay(s, a, x_sem.at[o, zz, a], (x + 1 + o) % cols, z, c))
        for a in range(3):
            act(relay(s, a, p_sem.at[0, zz, a], x, z, 1 - c))

    def spread_core(o, zz, act):
        s = slot((x + 1 + o) % cols, zz, c)
        last = depth - 1
        for a in range(3):
            up = ((z == 0) & along(1, zz, a)) | ((z == last - 1) & along(last, zz, a) & (zz == 0))
            down = ((z == last) & along(last - 1, zz, a)) | ((z == 1) & along(0, zz, a) & (zz == last))
            up = up & jnp.logical_not((z == 0) & (zz != 0))
            down = down & jnp.logical_not((z == last) & (zz != last))

            @pl.when(up)
            def _():
                act(relay(s, a, o_sem.at[o, zz, a], x, z + 1, c))

            @pl.when(down)
            def _():
                act(relay(s, a, o_sem.at[o, zz, a], x, z - 1, c))

        for a in range(3):
            act(relay(s, a, p_sem.at[1 + o, zz, a], x, z, 1 - c))

    def pick(s, e):
        chart_s = table[s].astype(jnp.float32)
        which = lax.broadcasted_iota(jnp.int32, chart_s.shape, 0) == e
        row = jnp.sum(jnp.where(which, chart_s, 0.0), axis=0, keepdims=True)
        off = lax.broadcasted_iota(jnp.int32, (rows, local), 1) - group * lax.broadcasted_iota(
            jnp.int32, (rows, local), 0
        )
        hit = (off >= 0) & (off < group) & (row > 0.0)
        return jnp.where(hit, 1.0, 0.0), row

    def send_ig(i, zz):
        xx = (x + i) % cols
        return send(
            igs.at[xx, zz], igb.at[xx, zz, c], igs_sem.at[xx, zz], igr_sem.at[xx, zz], x, z, 1 - c
        )

    def send_score(s):
        return pltpu.make_async_remote_copy(
            src_ref=scs.at[s],
            dst_ref=scr.at[me],
            send_sem=scs_sem.at[s],
            recv_sem=scr_sem.at[me],
            device_id={"da": s // depth, "db": s % depth},
            device_id_type=MESH,
        )

    span = local // PIECES

    def part(h):
        return pl.ds(h * span, span)

    def send_part(o, zz, h):
        return send(
            ps.at[o, zz, part(h)],
            pr.at[others - 1 - o, zz, part(h)],
            ps_sem.at[o, zz, h],
            pr_sem.at[others - 1 - o, zz, h],
            (x + 1 + o) % cols,
            z,
            c,
        )

    def send_row(zz, h):
        return send(rs.at[zz, part(h)], rz.at[z, part(h)], rs_sem.at[zz, h], rz_sem.at[z, h], x, zz, c)

    blocks = [(i, r) for i in range(cols) for r in range(CORES)]
    batch = len(blocks) * rows

    def compute(j, zz):
        base = pl.multiple_of(j * batch, batch)
        picks = []
        gate_cols = []
        for n, (i, r) in enumerate(blocks):
            s = slot((x + i) % cols, zz, (c + r) % CORES)
            chosen, row = pick(s, me)
            picks.append((s, chosen))
            gate_cols.append(jnp.sum(chosen * row, axis=1, keepdims=True))
            hot = chosen.astype(jnp.bfloat16)
            where = pl.ds(pl.multiple_of(base + n * rows, rows), rows)
            xs[where, :] = dot(hot, tok[s], ((1,), (0,))).astype(jnp.bfloat16)
            su[where, :] = dot(hot, up[s], ((1,), (0,))).astype(jnp.bfloat16)
        here = pl.ds(base, batch)
        gate = jnp.concatenate(gate_cols, axis=0)
        upstream = su[here, :]
        projected = dot(xs[here, :], win[...], ((1,), (0,)))
        back_raw = dot(upstream, wout[...], ((1,), (1,)))
        su[here, :] = (gate * upstream.astype(jnp.float32)).astype(jnp.bfloat16)
        gate_part, up_part = projected[:, :ff], projected[:, ff:]
        activated, derivative = silu_parts(gate_part)
        hidden = (activated * up_part).astype(jnp.bfloat16)
        hid[here, :] = hidden
        scores = jnp.sum(hidden.astype(jnp.float32) * back_raw, axis=1, keepdims=True)
        scores = scores.astype(jnp.bfloat16).astype(jnp.float32)
        back_hidden = gate * back_raw
        gp[here, :ff] = (back_hidden * up_part * derivative).astype(jnp.bfloat16)
        gp[here, ff:] = (back_hidden * activated).astype(jnp.bfloat16)
        grads = dot(gp[here, :], win[...], ((1,), (1,))).astype(jnp.bfloat16)
        for n, (i, r) in enumerate(blocks):
            xx = (x + i) % cols
            piece = grads[n * rows : (n + 1) * rows]
            if r == 0:
                igb[xx, zz, c] = piece
            else:
                igs[xx, zz] = piece
                send_ig(i, zz).start()
        for n, (i, r) in enumerate(blocks):
            s, chosen = picks[n]
            line = jnp.sum(chosen * scores[n * rows : (n + 1) * rows], axis=0, keepdims=True)
            scs[s] = jnp.broadcast_to(line, scs.shape[1:])
            if i == 0 and r == 0:

                @pl.when(zz == z)
                def _():
                    scr[me] = scs[me]

                @pl.when(zz != z)
                def _():
                    send_score(s).start()
            else:
                send_score(s).start()

    def chip_sum(i, zz):
        xx = (x + i) % cols
        s = slot(xx, zz, c)
        hot = jnp.concatenate([pick(s, slot(x, z, k))[0] for k in range(CORES)], axis=0)
        both = igb[xx, zz].reshape(CORES * rows, features)
        return dot(hot.astype(jnp.bfloat16), both, ((0,), (0,)))

    def start(copy):
        copy.start()

    def wait_send(copy):
        copy.wait_send()

    def step(i, carry):
        @pl.when(i < depth)
        def _():
            zz = visit(i, z, depth)

            @pl.when(i > 0)
            def _():
                arrive(slot(x, zz, c))

            spread_column(zz, start)

        @pl.when((i >= 2) & (i < depth + 2))
        def _():
            j = i - 2
            zz = visit(j, z, depth)

            @pl.when(j == 0)
            def _():
                loads[2].wait()
                loads[3].wait()

            for k in range(cols):
                arrive(slot((x + k) % cols, zz, 1 - c))
            compute(j, zz)
            for k in list(range(1, cols)) + [0]:
                send_ig(k, zz).wait_recv()
                total = chip_sum(k, zz)
                if k == 0:
                    pk[zz] = total
                else:
                    ps[k - 1, zz] = total.astype(jnp.bfloat16)
                    for h in range(PIECES):
                        send_part(k - 1, zz, h).start()

        @pl.when((i >= 1) & (i <= depth))
        def _():
            zz = visit(i - 1, z, depth)
            for o in range(others):
                arrive(slot((x + 1 + o) % cols, zz, c))
                spread_core(o, zz, start)

        @pl.when(i >= 4)
        def _():
            zz = visit(i - 4, z, depth)
            for h in range(PIECES):
                total = pk[zz, part(h)]
                for o in range(others):
                    send_part(others - 1 - o, zz, h).wait_recv()
                    total = total + pr[o, zz, part(h)].astype(jnp.float32)

                @pl.when(zz == z)
                def _():
                    rk[part(h), :] = total

                @pl.when(zz != z)
                def _():
                    rs[zz, part(h)] = total.astype(jnp.bfloat16)
                    send_row(zz, h).start()

        return carry

    lax.fori_loop(0, depth + 4, step, 0)

    wide = min(features, 256)

    @pl.loop(0, features // wide)
    def _(t):
        at = pl.ds(pl.multiple_of(t * wide, wide), wide)
        gin_ref[0, at, :] = dot(xs[:, at], gp[...], ((0,), (0,))).astype(jnp.bfloat16)

    thin = 128

    @pl.loop(0, ff // thin)
    def _(t):
        at = pl.ds(pl.multiple_of(t * thin, thin), thin)
        gdown_ref[0, at, :] = dot(hid[:, at], su[...], ((0,), (0,))).astype(jnp.bfloat16)

    @pl.loop(1, count)
    def _(k):
        s = (me + k) % count
        pltpu.make_async_remote_copy(
            src_ref=scs.at[s],
            dst_ref=scr.at[s],
            send_sem=scs_sem.at[s],
            recv_sem=scr_sem.at[s],
            device_id={"da": s // depth, "db": s % depth},
            device_id_type=MESH,
        ).wait()

    scores = scr[:, 0, :]
    place = lax.broadcasted_iota(jnp.int32, (top, local), 0)
    gate_grads = jnp.zeros((top, local), jnp.float32)
    for k in range(top):
        value = jnp.sum(jnp.where(routes[k : k + 1] == ids, scores, 0.0), axis=0, keepdims=True)
        gate_grads = jnp.where(place == k, value, gate_grads)
    gg_ref[...] = gate_grads.astype(jnp.bfloat16)

    def finish(k, carry):
        zz = (z + k) % depth
        for h in range(PIECES):
            send(
                rs.at[zz, part(h)], rz.at[zz, part(h)], rs_sem.at[zz, h], rz_sem.at[zz, h], x, zz, c
            ).wait()
            rk[part(h), :] += rz[zz, part(h)].astype(jnp.float32)
        return carry

    lax.fori_loop(1, depth, finish, 0)
    tg_ref[...] = rk[...].astype(jnp.bfloat16)

    def drain(zz, carry):
        spread_column(zz, wait_send)
        for o in range(others):
            spread_core(o, zz, wait_send)
            for h in range(PIECES):
                send_part(o, zz, h).wait_send()
        for k in range(cols):
            send_ig(k, zz).wait_send()
        return carry

    lax.fori_loop(0, depth, drain, 0)


def store_kernel(*refs):
    count = len(refs) // 2
    sems = refs[-1]
    copies = [
        pltpu.make_async_copy(refs[k], refs[count + k], sems.at[k]) for k in range(count)
    ]
    for one in copies:
        one.start()
    for one in copies:
        one.wait()


def store(*arrays):
    anywhere = pl.BlockSpec(memory_space=pl.ANY)
    return pl.pallas_call(
        store_kernel,
        out_shape=tuple(jax.ShapeDtypeStruct(a.shape, a.dtype) for a in arrays),
        in_specs=[pl.BlockSpec(memory_space=pltpu.VMEM)] * len(arrays),
        out_specs=(pl.BlockSpec(memory_space=pltpu.HBM),) * len(arrays),
        scratch_shapes=[pltpu.SemaphoreType.DMA((len(arrays),))],
        compiler_params=pltpu.CompilerParams(vmem_limit_bytes=8 * 2**20),
    )(*arrays)


def fused(tokens, grad_out, routes, gates, w_gate_up, w_down):
    first_size, depth = lax.axis_size("da"), lax.axis_size("db")
    cols = first_size // CORES
    experts = first_size * depth
    local, features = tokens.shape
    top = routes.shape[1]
    group = experts // top
    rows = local // group
    ff = w_down.shape[1]
    bf, f32 = jnp.bfloat16, jnp.float32
    total = rows * experts
    dma = pltpu.SemaphoreType.DMA
    scratch = [
        pltpu.VMEM((top, local), routes.dtype),
        pltpu.VMEM((top, local), gates.dtype),
        pltpu.VMEM((experts, local, features), bf),
        pltpu.VMEM((experts, local, features), bf),
        pltpu.VMEM((experts, experts, local), bf),
        pltpu.VMEM((features, 2 * ff), bf),
        pltpu.VMEM((ff, features), bf),
        pltpu.VMEM((total, features), bf),
        pltpu.VMEM((total, features), bf),
        pltpu.VMEM((total, ff), bf),
        pltpu.VMEM((total, 2 * ff), bf),
        pltpu.VMEM((cols, depth, rows, features), bf),
        pltpu.VMEM((cols, depth, CORES, rows, features), bf),
        pltpu.VMEM((cols - 1, depth, local, features), bf),
        pltpu.VMEM((depth, local, features), f32),
        pltpu.VMEM((cols - 1, depth, local, features), bf),
        pltpu.VMEM((depth, local, features), bf),
        pltpu.VMEM((local, features), f32),
        pltpu.VMEM((depth, local, features), bf),
        pltpu.VMEM((experts, 8, local), f32),
        pltpu.VMEM((experts, 8, local), f32),
        dma((6,)),
        dma((experts, 3)),
        dma((depth, 3)),
        dma((depth, 3)),
        dma((cols - 1, depth, 3)),
        dma((cols - 1, depth, 3)),
        dma((cols, depth, 3)),
        dma((cols, depth)),
        dma((cols, depth)),
        dma((cols - 1, depth, PIECES)),
        dma((cols - 1, depth, PIECES)),
        dma((depth, PIECES)),
        dma((depth, PIECES)),
        dma((experts,)),
        dma((experts,)),
    ]
    vmem = pl.BlockSpec(memory_space=pltpu.VMEM)
    hbm = pl.BlockSpec(memory_space=pltpu.HBM)
    token_grads, gate_grads, grad_in, grad_down = pl.pallas_call(
        functools.partial(fused_kernel, cols, depth, group),
        out_shape=(
            jax.ShapeDtypeStruct((local, features), bf),
            jax.ShapeDtypeStruct((top, local), bf),
            jax.ShapeDtypeStruct(w_gate_up.shape, bf),
            jax.ShapeDtypeStruct(w_down.shape, bf),
        ),
        in_specs=[hbm] * 6,
        out_specs=(vmem, vmem, vmem, vmem),
        scratch_shapes=scratch,
        compiler_params=pltpu.CompilerParams(
            collective_id=0, has_side_effects=True, vmem_limit_bytes=44 * 2**20
        ),
    )(
        *(
            pltpu.with_memory_space_constraint(a, pltpu.HBM)
            for a in (tokens, grad_out, routes.T, gates.T, w_gate_up, w_down)
        )
    )
    token_grads, gate_grads, grad_in, grad_down = store(token_grads, gate_grads, grad_in, grad_down)
    return token_grads, gate_grads.T, grad_in, grad_down


def fits(tokens, routes, w_down):
    first_size = lax.axis_size("da")
    experts = first_size * lax.axis_size("db")
    local, features = tokens.shape
    group = experts // routes.shape[1]
    held = 2 * experts * local * features * 2
    return (
        lax.axis_size("replica") == 1
        and first_size % CORES == 0
        and first_size > CORES
        and lax.axis_size("db") >= 4
        and held <= 16 * 2**20
        and local == 128
        and experts <= local
        and (local // group) % 16 == 0
        and w_down.shape[1] % 128 == 0
    )


def route(*arrays):
    if fits(arrays[0], arrays[2], arrays[5]):
        return fused(*arrays)
    return body(*arrays)


def solution(mesh):
    placed = (
        P(("groups", "replica", "da", "db"), None),
        P(("groups", "replica", "da", "db"), None),
        P(("groups", "replica", "da", "db"), None),
        P(("groups", "replica", "da", "db"), None),
        P(("da", "db"), "replica", None),
        P(("da", "db"), "replica", None),
    )
    return jax.shard_map(
        route,
        mesh=mesh,
        in_specs=placed,
        out_specs=(
            P(("groups", "replica", "da", "db"), None),
            P(("groups", "replica", "da", "db"), None),
            P(("groups", "da", "db"), "replica", None),
            P(("groups", "da", "db"), "replica", None),
        ),
        check_vma=False,
    )
```

```python
import functools

import jax
import jax.numpy as jnp
from jax import lax
from jax.experimental import pallas as pl
from jax.experimental.pallas import tpu as pltpu
from jax.sharding import PartitionSpec as P


CORES = 2
PIECES = 4
MESH = pl.DeviceIdType.MESH


def silu_parts(projected):
    sigmoid = jax.nn.sigmoid(projected)
    return (projected * sigmoid, sigmoid * (1.0 + projected * (1.0 - sigmoid)))


def body(tokens, grad_out, routes, gates, w_gate_up, w_down):
    local_tokens, features = tokens.shape
    top_count = routes.shape[1]
    hidden_units = w_gate_up.shape[2] // 2
    first_size = lax.axis_size("da")
    second_size = lax.axis_size("db")
    experts = first_size * second_size
    per_round = experts // top_count
    rounds = local_tokens // per_round
    expert_ids = lax.broadcasted_iota(jnp.int32, (1, 1, 1, experts), 3)
    matches = routes.reshape(rounds, per_round, top_count, 1) == expert_ids
    gate_values = gates.reshape(rounds, per_round, top_count, 1).astype(jnp.float32)
    gate_table = jnp.sum(jnp.where(matches, gate_values, 0.0), axis=(1, 2)).astype(jnp.bfloat16)
    chosen = jnp.any(matches, axis=2).astype(jnp.bfloat16)
    input_send = jnp.einsum(
        "rge,rgd->red",
        chosen,
        tokens.reshape(rounds, per_round, features),
        preferred_element_type=jnp.float32,
    ).astype(jnp.bfloat16)
    upstream_send = jnp.einsum(
        "rge,rgd->red",
        chosen,
        grad_out.reshape(rounds, per_round, features),
        preferred_element_type=jnp.float32,
    ).astype(jnp.bfloat16)
    input_recv, upstream_recv, gate_recv = (
        lax.all_to_all(input_send, ("da", "db"), split_axis=1, concat_axis=1, tiled=True),
        lax.all_to_all(upstream_send, ("da", "db"), split_axis=1, concat_axis=1, tiled=True),
        lax.all_to_all(gate_table, ("da", "db"), split_axis=1, concat_axis=1, tiled=True),
    )
    input_rows = input_recv.reshape(-1, features)
    upstream_rows = upstream_recv.reshape(-1, features)
    gate_rows = gate_recv.reshape(-1, 1).astype(jnp.float32)
    w_in, w_out = (
        lax.all_gather(w_gate_up[0], "replica", axis=0, tiled=True),
        lax.all_gather(w_down[0], "replica", axis=0, tiled=True),
    )
    projected = jnp.dot(input_rows, w_in, preferred_element_type=jnp.float32)
    back_raw = jnp.einsum("rd,fd->rf", upstream_rows, w_out, preferred_element_type=jnp.float32)
    gate_part = projected[:, :hidden_units]
    up_part = projected[:, hidden_units:]
    activated, derivative = silu_parts(gate_part)
    hidden = (activated * up_part).astype(jnp.bfloat16)
    gate_scores = jnp.sum(hidden.astype(jnp.float32) * back_raw, axis=1).astype(jnp.bfloat16)
    back_hidden = gate_rows * back_raw
    grad_projected = jnp.concatenate(
        [back_hidden * up_part * derivative, back_hidden * activated], axis=1
    ).astype(jnp.bfloat16)
    scaled_upstream = (gate_rows * upstream_rows.astype(jnp.float32)).astype(jnp.bfloat16)
    input_grads = jnp.einsum("rf,df->rd", grad_projected, w_in, preferred_element_type=jnp.float32)
    input_grads = input_grads.astype(jnp.bfloat16).reshape(rounds, experts, features)
    score_back = gate_scores.reshape(rounds, experts)
    returned, score_ret = (
        lax.all_to_all(input_grads, ("da", "db"), split_axis=1, concat_axis=1, tiled=True),
        lax.all_to_all(score_back, ("da", "db"), split_axis=1, concat_axis=1, tiled=True),
    )
    score_ret = score_ret.reshape(rounds, 1, 1, experts).astype(jnp.float32)
    token_grads = (
        jnp.einsum("rge,red->rgd", chosen, returned, preferred_element_type=jnp.float32)
        .astype(jnp.bfloat16)
        .reshape(local_tokens, features)
    )
    gate_grads = (
        jnp.sum(jnp.where(matches, score_ret, 0.0), axis=3)
        .astype(jnp.bfloat16)
        .reshape(local_tokens, top_count)
    )
    columns = input_rows
    grad_in = lax.psum_scatter(
        jnp.einsum("rd,rf->df", columns, grad_projected, preferred_element_type=jnp.float32).astype(
            jnp.bfloat16
        ),
        "replica",
        scatter_dimension=0,
        tiled=True,
    )
    columns = hidden
    grad_down = lax.psum_scatter(
        jnp.einsum(
            "rf,rd->fd", columns, scaled_upstream, preferred_element_type=jnp.float32
        ).astype(jnp.bfloat16),
        "replica",
        scatter_dimension=0,
        tiled=True,
    )
    return (token_grads, gate_grads, grad_in[None], grad_down[None])


def visit(j, z, n):
    m = jnp.minimum(z, n - 1 - z)
    near = z + (1 - 2 * (j % 2)) * ((j + 1) // 2)
    far = jnp.where(z < n - 1 - z, j, n - 1 - j)
    return jnp.where(j <= 2 * m, near, far)


def dot(a, b, dims):
    return lax.dot_general(a, b, (dims, ((), ())), preferred_element_type=jnp.float32)


def fused_kernel(
    cols, depth, group,
    tok_hbm, up_hbm, routes_hbm, gates_hbm, win_hbm, wout_hbm,
    tg_ref, gg_ref, gin_ref, gdown_ref,
    routes_ref, gates_ref, tok, up, table, win, wout, xs, su, hid, gp, igs, igb, ps, pk, pr, rs, rk, rz, scs, scr,
    load_sem, recv_sem, zup_sem, zdn_sem, x_sem, o_sem, p_sem, igs_sem, igr_sem, ps_sem, pr_sem, rs_sem, rz_sem,
    scs_sem, scr_sem,
):
    da = lax.axis_index("da")
    z = lax.axis_index("db")
    x, c = da // CORES, da % CORES
    local, features = tok.shape[1], tok.shape[2]
    experts = table.shape[1]
    top = routes_ref.shape[0]
    rows = local // group
    ff = wout.shape[0]
    others = cols - 1

    def slot(xx, zz, cc):
        return (xx * CORES + cc) * depth + zz

    me = slot(x, z, c)
    loads = [
        pltpu.make_async_copy(tok_hbm, tok.at[me], load_sem.at[0]),
        pltpu.make_async_copy(up_hbm, up.at[me], load_sem.at[1]),
        pltpu.make_async_copy(win_hbm.at[0], win, load_sem.at[2]),
        pltpu.make_async_copy(wout_hbm.at[0], wout, load_sem.at[3]),
        pltpu.make_async_copy(routes_hbm, routes_ref, load_sem.at[4]),
        pltpu.make_async_copy(gates_hbm, gates_ref, load_sem.at[5]),
    ]
    for k in (4, 5, 0, 1, 2, 3):
        loads[k].start()

    barrier = pltpu.get_barrier_semaphore()
    count = cols * CORES * depth

    @pl.loop(1, count)
    def _(k):
        to = (me + k) % count
        pl.semaphore_signal(
            barrier, inc=1, device_id={"da": to // depth, "db": to % depth}, device_id_type=MESH
        )

    loads[4].wait()
    loads[5].wait()
    routes = routes_ref[...]
    gates = gates_ref[...].astype(jnp.float32)
    ids = lax.broadcasted_iota(jnp.int32, (experts, local), 0)
    chart = jnp.zeros((experts, local), jnp.float32)
    for k in range(top):
        chart = chart + jnp.where(routes[k : k + 1] == ids, gates[k : k + 1], 0.0)
    table[me] = chart.astype(jnp.bfloat16)

    pl.semaphore_wait(barrier, count - 1)
    loads[0].wait()
    loads[1].wait()

    held = (table, tok, up)

    def send(src, dst, send_sem, recv, to_x, to_z, to_c):
        return pltpu.make_async_remote_copy(
            src_ref=src,
            dst_ref=dst,
            send_sem=send_sem,
            recv_sem=recv,
            device_id={"da": to_x * CORES + to_c, "db": to_z},
            device_id_type=MESH,
        )

    def relay(s, a, sem, to_x, to_z, to_c):
        ref = held[a].at[s]
        return send(ref, ref, sem, recv_sem.at[s, a], to_x, to_z, to_c)

    def arrive(s):
        for a in range(3):
            relay(s, a, p_sem.at[0, 0, a], x, z, 1 - c).wait_recv()

    def along(row, zz, a):
        last = depth - 1
        near = ((row == 1) & (zz == 0)) | ((row == last - 1) & (zz == last))
        if a != 2:
            return near
        return near | ((row == 0) & (zz == last)) | ((row == last) & (zz == 0))

    def spread_column(zz, act, await_first=None):
        s = slot(x, zz, c)
        for a in range(3):
            if await_first is not None:

                @pl.when(await_first)
                def _():
                    relay(s, a, p_sem.at[0, 0, a], x, z, 1 - c).wait_recv()

            @pl.when((zz <= z) & (z < depth - 1))
            def _():
                act(relay(s, a, zup_sem.at[zz, a], x, z + 1, c))

            @pl.when((zz >= z) & (z > 0))
            def _():
                act(relay(s, a, zdn_sem.at[zz, a], x, z - 1, c))

            for o in range(others):

                @pl.when(jnp.logical_not(along(z, zz, a)))
                def _():
                    act(relay(s, a, x_sem.at[o, zz, a], (x + 1 + o) % cols, z, c))

            act(relay(s, a, p_sem.at[0, zz, a], x, z, 1 - c))

    def spread_core(o, zz, act):
        s = slot((x + 1 + o) % cols, zz, c)
        last = depth - 1
        for a in range(3):
            up = ((z == 0) & along(1, zz, a)) | ((z == last - 1) & along(last, zz, a) & (zz == 0))
            down = ((z == last) & along(last - 1, zz, a)) | ((z == 1) & along(0, zz, a) & (zz == last))
            up = up & jnp.logical_not((z == 0) & (zz != 0))
            down = down & jnp.logical_not((z == last) & (zz != last))

            @pl.when(up)
            def _():
                act(relay(s, a, o_sem.at[o, zz, a], x, z + 1, c))

            @pl.when(down)
            def _():
                act(relay(s, a, o_sem.at[o, zz, a], x, z - 1, c))

        for a in range(3):
            act(relay(s, a, p_sem.at[1 + o, zz, a], x, z, 1 - c))

    def pick(s, e):
        chart_s = table[s].astype(jnp.float32)
        which = lax.broadcasted_iota(jnp.int32, chart_s.shape, 0) == e
        row = jnp.sum(jnp.where(which, chart_s, 0.0), axis=0, keepdims=True)
        off = lax.broadcasted_iota(jnp.int32, (rows, local), 1) - group * lax.broadcasted_iota(
            jnp.int32, (rows, local), 0
        )
        hit = (off >= 0) & (off < group) & (row > 0.0)
        return jnp.where(hit, 1.0, 0.0), row

    def send_ig(i, zz):
        xx = (x + i) % cols
        return send(
            igs.at[xx, zz], igb.at[xx, zz, c], igs_sem.at[xx, zz], igr_sem.at[xx, zz], x, z, 1 - c
        )

    def send_score(s):
        return pltpu.make_async_remote_copy(
            src_ref=scs.at[s],
            dst_ref=scr.at[me],
            send_sem=scs_sem.at[s],
            recv_sem=scr_sem.at[me],
            device_id={"da": s // depth, "db": s % depth},
            device_id_type=MESH,
        )

    span = local // PIECES

    def part(h):
        return pl.ds(h * span, span)

    def send_part(o, zz, h):
        return send(
            ps.at[o, zz, part(h)],
            pr.at[others - 1 - o, zz, part(h)],
            ps_sem.at[o, zz, h],
            pr_sem.at[others - 1 - o, zz, h],
            (x + 1 + o) % cols,
            z,
            c,
        )

    def send_row(zz, h):
        return send(rs.at[zz, part(h)], rz.at[z, part(h)], rs_sem.at[zz, h], rz_sem.at[z, h], x, zz, c)

    blocks = [(i, r) for i in range(cols) for r in range(CORES)]
    batch = len(blocks) * rows

    def compute(j, zz):
        base = pl.multiple_of(j * batch, batch)
        picks = []
        gate_cols = []
        for n, (i, r) in enumerate(blocks):
            s = slot((x + i) % cols, zz, (c + r) % CORES)
            chosen, row = pick(s, me)
            picks.append((s, chosen))
            gate_cols.append(jnp.sum(chosen * row, axis=1, keepdims=True))
            hot = chosen.astype(jnp.bfloat16)
            where = pl.ds(pl.multiple_of(base + n * rows, rows), rows)
            xs[where, :] = dot(hot, tok[s], ((1,), (0,))).astype(jnp.bfloat16)
            su[where, :] = dot(hot, up[s], ((1,), (0,))).astype(jnp.bfloat16)
        here = pl.ds(base, batch)
        gate = jnp.concatenate(gate_cols, axis=0)
        upstream = su[here, :]
        projected = dot(xs[here, :], win[...], ((1,), (0,)))
        back_raw = dot(upstream, wout[...], ((1,), (1,)))
        su[here, :] = (gate * upstream.astype(jnp.float32)).astype(jnp.bfloat16)
        gate_part, up_part = projected[:, :ff], projected[:, ff:]
        activated, derivative = silu_parts(gate_part)
        hidden = (activated * up_part).astype(jnp.bfloat16)
        hid[here, :] = hidden
        scores = jnp.sum(hidden.astype(jnp.float32) * back_raw, axis=1, keepdims=True)
        scores = scores.astype(jnp.bfloat16).astype(jnp.float32)
        back_hidden = gate * back_raw
        gp[here, :ff] = (back_hidden * up_part * derivative).astype(jnp.bfloat16)
        gp[here, ff:] = (back_hidden * activated).astype(jnp.bfloat16)
        grads = dot(gp[here, :], win[...], ((1,), (1,))).astype(jnp.bfloat16)
        for n, (i, r) in enumerate(blocks):
            xx = (x + i) % cols
            piece = grads[n * rows : (n + 1) * rows]
            if r == 0:
                igb[xx, zz, c] = piece
            else:
                igs[xx, zz] = piece
                send_ig(i, zz).start()
        for n, (i, r) in enumerate(blocks):
            s, chosen = picks[n]
            line = jnp.sum(chosen * scores[n * rows : (n + 1) * rows], axis=0, keepdims=True)
            scs[s] = jnp.broadcast_to(line, scs.shape[1:])
            if i == 0 and r == 0:

                @pl.when(zz == z)
                def _():
                    scr[me] = scs[me]

                @pl.when(zz != z)
                def _():
                    send_score(s).start()
            else:
                send_score(s).start()

    def chip_sum(i, zz):
        xx = (x + i) % cols
        s = slot(xx, zz, c)
        hot = jnp.concatenate([pick(s, slot(x, z, k))[0] for k in range(CORES)], axis=0)
        both = igb[xx, zz].reshape(CORES * rows, features)
        return dot(hot.astype(jnp.bfloat16), both, ((0,), (0,)))

    def start(copy):
        copy.start()

    def wait_send(copy):
        copy.wait_send()

    def step(i, carry):
        @pl.when(i < depth)
        def _():
            zz = visit(i, z, depth)

            spread_column(zz, start, i > 0)

        @pl.when((i >= 2) & (i < depth + 2))
        def _():
            j = i - 2
            zz = visit(j, z, depth)

            @pl.when(j == 0)
            def _():
                loads[2].wait()
                loads[3].wait()

            for k in range(cols):
                arrive(slot((x + k) % cols, zz, 1 - c))
            compute(j, zz)
            for k in list(range(1, cols)) + [0]:
                send_ig(k, zz).wait_recv()
                total = chip_sum(k, zz)
                if k == 0:
                    pk[zz] = total
                else:
                    ps[k - 1, zz] = total.astype(jnp.bfloat16)
                    for h in range(PIECES):
                        send_part(k - 1, zz, h).start()

        @pl.when((i >= 1) & (i <= depth))
        def _():
            zz = visit(i - 1, z, depth)
            for o in range(others):
                arrive(slot((x + 1 + o) % cols, zz, c))
                spread_core(o, zz, start)

        @pl.when(i >= 4)
        def _():
            zz = visit(i - 4, z, depth)
            for h in range(PIECES):
                total = pk[zz, part(h)]
                for o in range(others):
                    send_part(others - 1 - o, zz, h).wait_recv()
                    total = total + pr[o, zz, part(h)].astype(jnp.float32)

                @pl.when(zz == z)
                def _():
                    rk[part(h), :] = total

                @pl.when(zz != z)
                def _():
                    rs[zz, part(h)] = total.astype(jnp.bfloat16)
                    send_row(zz, h).start()

        return carry

    lax.fori_loop(0, depth + 4, step, 0)

    wide = min(features, 256)

    @pl.loop(0, features // wide)
    def _(t):
        at = pl.ds(pl.multiple_of(t * wide, wide), wide)
        gin_ref[0, at, :] = dot(xs[:, at], gp[...], ((0,), (0,))).astype(jnp.bfloat16)

    thin = 128

    @pl.loop(0, ff // thin)
    def _(t):
        at = pl.ds(pl.multiple_of(t * thin, thin), thin)
        gdown_ref[0, at, :] = dot(hid[:, at], su[...], ((0,), (0,))).astype(jnp.bfloat16)

    @pl.loop(1, count)
    def _(k):
        s = (me + k) % count
        pltpu.make_async_remote_copy(
            src_ref=scs.at[s],
            dst_ref=scr.at[s],
            send_sem=scs_sem.at[s],
            recv_sem=scr_sem.at[s],
            device_id={"da": s // depth, "db": s % depth},
            device_id_type=MESH,
        ).wait()

    scores = scr[:, 0, :]
    place = lax.broadcasted_iota(jnp.int32, (top, local), 0)
    gate_grads = jnp.zeros((top, local), jnp.float32)
    for k in range(top):
        value = jnp.sum(jnp.where(routes[k : k + 1] == ids, scores, 0.0), axis=0, keepdims=True)
        gate_grads = jnp.where(place == k, value, gate_grads)
    gg_ref[...] = gate_grads.astype(jnp.bfloat16)

    def finish(k, carry):
        zz = (z + k) % depth
        for h in range(PIECES):
            send(
                rs.at[zz, part(h)], rz.at[zz, part(h)], rs_sem.at[zz, h], rz_sem.at[zz, h], x, zz, c
            ).wait()
            rk[part(h), :] += rz[zz, part(h)].astype(jnp.float32)
        return carry

    lax.fori_loop(1, depth, finish, 0)
    tg_ref[...] = rk[...].astype(jnp.bfloat16)

    def drain(zz, carry):
        spread_column(zz, wait_send)
        for o in range(others):
            spread_core(o, zz, wait_send)
            for h in range(PIECES):
                send_part(o, zz, h).wait_send()
        for k in range(cols):
            send_ig(k, zz).wait_send()
        return carry

    lax.fori_loop(0, depth, drain, 0)


def store_kernel(*refs):
    count = len(refs) // 2
    sems = refs[-1]
    copies = [
        pltpu.make_async_copy(refs[k], refs[count + k], sems.at[k]) for k in range(count)
    ]
    for one in copies:
        one.start()
    for one in copies:
        one.wait()


def store(*arrays):
    anywhere = pl.BlockSpec(memory_space=pl.ANY)
    return pl.pallas_call(
        store_kernel,
        out_shape=tuple(jax.ShapeDtypeStruct(a.shape, a.dtype) for a in arrays),
        in_specs=[pl.BlockSpec(memory_space=pltpu.VMEM)] * len(arrays),
        out_specs=(pl.BlockSpec(memory_space=pltpu.HBM),) * len(arrays),
        scratch_shapes=[pltpu.SemaphoreType.DMA((len(arrays),))],
        compiler_params=pltpu.CompilerParams(vmem_limit_bytes=8 * 2**20),
    )(*arrays)


def fused(tokens, grad_out, routes, gates, w_gate_up, w_down):
    first_size, depth = lax.axis_size("da"), lax.axis_size("db")
    cols = first_size // CORES
    experts = first_size * depth
    local, features = tokens.shape
    top = routes.shape[1]
    group = experts // top
    rows = local // group
    ff = w_down.shape[1]
    bf, f32 = jnp.bfloat16, jnp.float32
    total = rows * experts
    dma = pltpu.SemaphoreType.DMA
    scratch = [
        pltpu.VMEM((top, local), routes.dtype),
        pltpu.VMEM((top, local), gates.dtype),
        pltpu.VMEM((experts, local, features), bf),
        pltpu.VMEM((experts, local, features), bf),
        pltpu.VMEM((experts, experts, local), bf),
        pltpu.VMEM((features, 2 * ff), bf),
        pltpu.VMEM((ff, features), bf),
        pltpu.VMEM((total, features), bf),
        pltpu.VMEM((total, features), bf),
        pltpu.VMEM((total, ff), bf),
        pltpu.VMEM((total, 2 * ff), bf),
        pltpu.VMEM((cols, depth, rows, features), bf),
        pltpu.VMEM((cols, depth, CORES, rows, features), bf),
        pltpu.VMEM((cols - 1, depth, local, features), bf),
        pltpu.VMEM((depth, local, features), f32),
        pltpu.VMEM((cols - 1, depth, local, features), bf),
        pltpu.VMEM((depth, local, features), bf),
        pltpu.VMEM((local, features), f32),
        pltpu.VMEM((depth, local, features), bf),
        pltpu.VMEM((experts, 8, local), f32),
        pltpu.VMEM((experts, 8, local), f32),
        dma((6,)),
        dma((experts, 3)),
        dma((depth, 3)),
        dma((depth, 3)),
        dma((cols - 1, depth, 3)),
        dma((cols - 1, depth, 3)),
        dma((cols, depth, 3)),
        dma((cols, depth)),
        dma((cols, depth)),
        dma((cols - 1, depth, PIECES)),
        dma((cols - 1, depth, PIECES)),
        dma((depth, PIECES)),
        dma((depth, PIECES)),
        dma((experts,)),
        dma((experts,)),
    ]
    vmem = pl.BlockSpec(memory_space=pltpu.VMEM)
    hbm = pl.BlockSpec(memory_space=pltpu.HBM)
    token_grads, gate_grads, grad_in, grad_down = pl.pallas_call(
        functools.partial(fused_kernel, cols, depth, group),
        out_shape=(
            jax.ShapeDtypeStruct((local, features), bf),
            jax.ShapeDtypeStruct((top, local), bf),
            jax.ShapeDtypeStruct(w_gate_up.shape, bf),
            jax.ShapeDtypeStruct(w_down.shape, bf),
        ),
        in_specs=[hbm] * 6,
        out_specs=(vmem, vmem, vmem, vmem),
        scratch_shapes=scratch,
        compiler_params=pltpu.CompilerParams(
            collective_id=0, has_side_effects=True, vmem_limit_bytes=44 * 2**20
        ),
    )(
        *(
            pltpu.with_memory_space_constraint(a, pltpu.HBM)
            for a in (tokens, grad_out, routes.T, gates.T, w_gate_up, w_down)
        )
    )
    token_grads, gate_grads, grad_in, grad_down = store(token_grads, gate_grads, grad_in, grad_down)
    return token_grads, gate_grads.T, grad_in, grad_down


def fits(tokens, routes, w_down):
    first_size = lax.axis_size("da")
    experts = first_size * lax.axis_size("db")
    local, features = tokens.shape
    group = experts // routes.shape[1]
    held = 2 * experts * local * features * 2
    return (
        lax.axis_size("replica") == 1
        and first_size % CORES == 0
        and first_size > CORES
        and lax.axis_size("db") >= 4
        and held <= 16 * 2**20
        and local == 128
        and experts <= local
        and (local // group) % 16 == 0
        and w_down.shape[1] % 128 == 0
    )


def route(*arrays):
    if fits(arrays[0], arrays[2], arrays[5]):
        return fused(*arrays)
    return body(*arrays)


def solution(mesh):
    placed = (
        P(("groups", "replica", "da", "db"), None),
        P(("groups", "replica", "da", "db"), None),
        P(("groups", "replica", "da", "db"), None),
        P(("groups", "replica", "da", "db"), None),
        P(("da", "db"), "replica", None),
        P(("da", "db"), "replica", None),
    )
    return jax.shard_map(
        route,
        mesh=mesh,
        in_specs=placed,
        out_specs=(
            P(("groups", "replica", "da", "db"), None),
            P(("groups", "replica", "da", "db"), None),
            P(("groups", "da", "db"), "replica", None),
            P(("groups", "da", "db"), "replica", None),
        ),
        check_vma=False,
    )
```
